512 devices in a mesh: tm: 16 (over y, z_lo), feed: 32 (over z_hi, x, core).
Axes of the slice: x: 4, y: 8, z: 8 (z_hi: 4, z_lo: 2; z = z_hi * 2 + z_lo), core: 2. Of those that a mesh axis runs over, the one named last changes fastest.
Arguments:
- voltages: int32 [2048, 131072], P('feed', 'tm'), may hold values from -128 to 127
- feed_at_grid_slot: int32 [2048], replicated, may hold values from 0 to 2047, each once
- ew_grid: int32 [4], replicated, may hold values from 0 to 511
- ns_grid: int32 [256], replicated, may hold values from 0 to 511
- delays: int32 [1024, 512], replicated, may hold values from 0 to 63, as said below
Outputs:
- dedispersed: float32 [512, 1024, 64], P('tm', 'feed')
The draws below stay inside these ranges and needn't reach their ends.
Inputs may be any that keep to these rules, and one draw needn't show every extreme that they name: `feed_at_grid_slot`: each feed stands at exactly one grid position. delays are taken modulo 64.
All inputs are finite; a program needn't handle non-finite values.
Results may differ from the reference program's by a relative error of at most 0.017.
Values may be sent and summed in bfloat16 or wider, within the bound.
No kernel may reach another device: no remote copies, remote signals or barrier semaphores. Data moves between devices by JAX's collectives and lax.ppermute only.
A program may use at most 64 MiB of HBM per device.

```python
import math
from functools import partial
import jax
import jax.numpy as jnp
from jax import lax

NFFT = 2048
CHANS = 1024
TAPS = 4
ROWS = 256
FEEDS = 2048
NS_BEAMS = 256
EW_BEAMS = 4
BEAMS = 1024
DMS = 512
SPECTRA = 64


def draw_delays(key, part):
    dm_key = jax.random.fold_in(key, 11)
    lag_key = jax.random.fold_in(key, 12)
    trials = jnp.arange(DMS, dtype=jnp.int32) * 4 + jax.random.randint(dm_key, (DMS,), 0, 4, dtype=jnp.int32)
    chan_ids = jnp.arange(CHANS, dtype=jnp.int32) + CHANS
    sweep_rate = 1073741824 // (chan_ids * chan_ids)
    offsets = jax.random.randint(lag_key, (CHANS,), 0, SPECTRA, dtype=jnp.int32)
    sweep_lag = jnp.right_shift(trials[None, :] * sweep_rate[:, None], 12)
    return (sweep_lag + offsets[:, None]) % SPECTRA


def touch_ends(entries, rng, least, largest):
    spot = [jax.random.randint(jax.random.fold_in(rng, axis), (), 0, length) for axis, length in enumerate(entries.shape)]
    widest = entries.shape.index(max(entries.shape))
    neighbour = spot[:widest] + [(spot[widest] + 1) % entries.shape[widest]] + spot[widest + 1:]
    return entries.at[tuple(spot)].set(least).at[tuple(neighbour)].set(largest)


def setup_inputs(seed: int = 0) -> dict:
    keys = jax.random.split(jax.random.key(seed), 6)
    return {
        "voltages": touch_ends(jax.random.randint(keys[0], (FEEDS, SPECTRA * NFFT), -128, 128), jax.random.fold_in(keys[0], 1), -128, 127).astype(jnp.int32),
        "feed_at_grid_slot": jax.random.permutation(keys[1], FEEDS).astype(jnp.int32),
        "ew_grid": touch_ends(jax.random.randint(keys[2], (EW_BEAMS,), 0, 512), jax.random.fold_in(keys[2], 1), 0, 511).astype(jnp.int32),
        "ns_grid": touch_ends(jax.random.randint(keys[3], (NS_BEAMS,), 0, 512), jax.random.fold_in(keys[3], 1), 0, 511).astype(jnp.int32),
        "delays": draw_delays(jax.random.fold_in(keys[5], 71), 0),
    }


TWO_PI = 2.0 * math.pi
phase_modulus = 1048576

def rounded_value(values):
    return lax.optimization_barrier(values.astype(jnp.bfloat16)).astype(jnp.float32)

def pfb_window(tap_count, series_length):
    points = jnp.arange(tap_count * series_length, dtype=jnp.float32) + 0.5
    start_offset = points / series_length - tap_count / 2.0
    taper = 0.5 - 0.5 * jnp.cos(TWO_PI * points / (tap_count * series_length))
    values = (jnp.sinc(start_offset) * taper).reshape(tap_count, series_length)
    return values / jnp.sqrt(lax.optimization_barrier(jnp.sum(values * values, axis=0, keepdims=True)))

def dft_table(series_length, columns):
    product = jnp.arange(series_length, dtype=jnp.int32)[:, None] * jnp.arange(columns, dtype=jnp.int32)[None, :] % series_length
    angles = product.astype(jnp.float32) * (TWO_PI / series_length)
    factor = 1.0 / math.sqrt(series_length)
    return jnp.concatenate([jnp.cos(angles) * factor, -jnp.sin(angles) * factor], axis=1).astype(jnp.bfloat16)

def spectral_table(series_length):
    product = jnp.arange(series_length, dtype=jnp.int32)[:, None] * jnp.arange(series_length, dtype=jnp.int32)[None, :] % series_length
    angles = product.astype(jnp.float32) * (TWO_PI / series_length)
    factor = 1.0 / math.sqrt(series_length)
    nonzero = (jnp.arange(series_length) > 0)[:, None]
    cosine = jnp.where(nonzero, jnp.cos(angles) * factor, 0.0)
    sine_part = jnp.where(nonzero, -jnp.sin(angles) * factor, 0.0)
    return jnp.stack([cosine, sine_part]).astype(jnp.bfloat16)

def steer_table(coords, grid_ids, chan_ids, factor):
    phases = coords[None, None, :] * grid_ids[None, :, None] * chan_ids[:, None, None] % phase_modulus
    angles = phases.astype(jnp.float32) * (TWO_PI / phase_modulus)
    return ((jnp.cos(angles) * factor).astype(jnp.bfloat16), (jnp.sin(angles) * factor).astype(jnp.bfloat16))

def form_beams(block_in, feed_at_grid_slot, ew_tables, ns_tables):
    ew_real = ew_tables[0].astype(jnp.float32)
    ew_imag = ew_tables[1].astype(jnp.float32)
    ns_real = ns_tables[0].astype(jnp.float32)
    ns_imag = ns_tables[1].astype(jnp.float32)
    item_count = block_in.shape[1]
    chan_count = block_in.shape[3]
    gridded = jnp.take(block_in, feed_at_grid_slot, axis=0).reshape(ROWS, 4, 2, item_count, 2, chan_count)
    grid_real = gridded[:, :, :, :, 0, :].astype(jnp.float32)
    grid_imag = gridded[:, :, :, :, 1, :].astype(jnp.float32)
    east_mix = partial(jnp.einsum, 'cey,rypsc->erpsc')
    east_real = rounded_value(east_mix(ew_real, grid_real) - east_mix(ew_imag, grid_imag))
    east_imag = rounded_value(east_mix(ew_real, grid_imag) + east_mix(ew_imag, grid_real))
    north_mix = partial(jnp.einsum, 'cbr,erpsc->ebpsc')
    beam_real = north_mix(ns_real, east_real) - north_mix(ns_imag, east_imag)
    beam_imag = north_mix(ns_real, east_imag) + north_mix(ns_imag, east_real)
    beam_power = lax.optimization_barrier(jnp.sum(beam_real * beam_real + beam_imag * beam_imag, axis=2))
    return beam_power.reshape(-1, item_count, chan_count).astype(jnp.bfloat16)

def reference(voltages, feed_at_grid_slot, ew_grid, ns_grid, delays):
    spec_total = voltages.shape[1] // NFFT
    window = pfb_window(TAPS, NFFT)
    twiddle = dft_table(NFFT, CHANS)
    feeds_per_block = math.gcd(FEEDS, 64)

    def channelize(block_in):
        frames = (block_in.astype(jnp.float32) / 64.0).astype(jnp.bfloat16).reshape(feeds_per_block, spec_total, NFFT)
        padded = jnp.concatenate([jnp.zeros((feeds_per_block, TAPS - 1, NFFT), jnp.bfloat16), frames], axis=1)
        filtered = jnp.zeros((feeds_per_block, spec_total, NFFT), jnp.float32)
        for tap_index in range(TAPS):
            filtered = filtered + window[tap_index] * padded[:, tap_index:tap_index + spec_total, :].astype(jnp.float32)
        result = jnp.dot(filtered.astype(jnp.bfloat16).reshape(-1, NFFT), twiddle, preferred_element_type=jnp.float32)
        return result.astype(jnp.bfloat16).reshape(feeds_per_block, spec_total, 2, CHANS)
    spectra = lax.map(channelize, voltages.reshape(FEEDS // feeds_per_block, feeds_per_block, -1))
    spectra = spectra.reshape(FEEDS, spec_total, 2, CHANS)
    chan_block = math.gcd(CHANS, 32)
    block_count = CHANS // chan_block
    gridded_everything = spectra.reshape(FEEDS, spec_total, 2, block_count, chan_block).transpose(3, 0, 1, 2, 4)

    def beam_block(inputs):
        chan_part, chan_start = inputs
        chan_ids = chan_start + jnp.arange(chan_block, dtype=jnp.int32) + CHANS
        ew_tables = steer_table(jnp.arange(4, dtype=jnp.int32), ew_grid, chan_ids, 0.5)
        ns_tables = steer_table(jnp.arange(ROWS, dtype=jnp.int32), ns_grid, chan_ids, 1.0 / math.sqrt(ROWS))
        return form_beams(chan_part, feed_at_grid_slot, ew_tables, ns_tables)
    starts = jnp.arange(block_count, dtype=jnp.int32) * chan_block
    powers = lax.map(beam_block, (gridded_everything, starts))
    intensity = powers.transpose(1, 2, 0, 3).reshape(BEAMS, spec_total, CHANS)
    time_wide = spectral_table(spec_total).astype(jnp.float32)
    freq_ids = jnp.arange(spec_total, dtype=jnp.int32)
    phases = freq_ids[:, None, None] * delays[None, :, :] % spec_total
    angles = phases.astype(jnp.float32) * (TWO_PI / spec_total)
    phase_real = rounded_value(jnp.cos(angles))
    phase_imag = rounded_value(jnp.sin(angles))
    shift_mixture = partial(jnp.einsum, 'vuw,uwt->vut')
    beam_block_size = math.gcd(BEAMS, 32)

    def search(block_in):
        freq_part = rounded_value(jnp.einsum('rkt,btc->brkc', time_wide, block_in.astype(jnp.float32)))
        spec_real = freq_part[:, 0]
        spec_imag = freq_part[:, 1]
        moved_real = shift_mixture(spec_real, phase_real) - shift_mixture(spec_imag, phase_imag)
        moved_imag = shift_mixture(spec_real, phase_imag) + shift_mixture(spec_imag, phase_real)
        folded = rounded_value(jnp.stack([moved_real, moved_imag], axis=1) * (1.0 / math.sqrt(CHANS)))
        return jnp.einsum('brkd,rkt->dbt', folded, time_wide)
    searched = lax.map(search, intensity.reshape(-1, beam_block_size, spec_total, CHANS))
    return searched.transpose(1, 0, 2, 3).reshape(DMS, BEAMS, spec_total)
```

```python
import math
from functools import partial

import jax
import jax.numpy as jnp
from jax import lax
from jax.experimental import pallas as pl
from jax.experimental.pallas import tpu as pltpu
from jax.sharding import PartitionSpec as P

NFFT = 2048
CHANS = 1024
TAPS = 4
ROWS = 256
SPECTRA = 64
HALF = NFFT // 2
TWO_PI = 2.0 * math.pi
PHASE_MODULUS = 1048576
F32 = jnp.float32
BF16 = jnp.bfloat16
NT = (((1,), (1,)), ((), ()))


def iota(shape, axis):
    return lax.broadcasted_iota(jnp.int32, shape, axis)


def pfb_window():
    points = jnp.arange(TAPS * NFFT, dtype=F32) + 0.5
    start_offset = points / NFFT - TAPS / 2.0
    taper = 0.5 - 0.5 * jnp.cos(TWO_PI * points / (TAPS * NFFT))
    values = (jnp.sinc(start_offset) * taper).reshape(TAPS, NFFT)
    return values / jnp.sqrt(jnp.sum(values * values, axis=0, keepdims=True))


def twiddle_tables():
    coarse = iota((32, HALF), 0) * iota((32, HALF), 1) % 64
    coarse = coarse.astype(F32) * (TWO_PI / 64)
    shape = (2, 32, HALF)
    row = iota(shape, 1)
    chan = (row // 2) * 2 + iota(shape, 0)
    fine = (chan * iota(shape, 2) + (row % 2) * 512) % NFFT
    fine = fine.astype(F32) * (TWO_PI / NFFT)
    factor = 1.0 / math.sqrt(NFFT)
    seeds = (jnp.cos(coarse), jnp.sin(coarse), jnp.cos(fine) * factor, jnp.sin(fine) * factor)
    cos_a, sin_a, cos_b, sin_b = lax.optimization_barrier(seeds)
    table = cos_a[None, :, None, :] * cos_b[:, None] - sin_a[None, :, None, :] * sin_b[:, None]
    return table.astype(BF16).reshape(2, 1024, HALF)


def steer_seed(steps, grid_ids, chan_ids, factor):
    phases = steps[None, :, None] * grid_ids[None, None, :] * chan_ids[:, None, None] % PHASE_MODULUS
    angles = phases.astype(F32) * (TWO_PI / PHASE_MODULUS)
    return jnp.cos(angles) * factor, jnp.sin(angles) * factor


def north_tables(ns_grid, chan_ids):
    steps = jnp.arange(16, dtype=jnp.int32)
    seeds = steer_seed(steps * 16, ns_grid, chan_ids, 1.0) + steer_seed(steps, ns_grid, chan_ids, 1.0 / math.sqrt(ROWS))
    cos_a, sin_a, cos_b, sin_b = lax.optimization_barrier(seeds)
    cos_a, sin_a = cos_a[:, :, None, :], sin_a[:, :, None, :]
    cos_b, sin_b = cos_b[:, None], sin_b[:, None]
    real = (cos_a * cos_b - sin_a * sin_b).astype(BF16).reshape(2, ROWS, 256)
    imag = (sin_a * cos_b + cos_a * sin_b).astype(BF16).reshape(2, ROWS, 256)
    return jnp.concatenate([real, imag], axis=2)


def time_rows():
    block = jnp.arange(16, dtype=jnp.int32)
    ks = jnp.stack([block + 1, jnp.where(block == 15, 32, 31 - block)])
    product = ks[:, :, None] * jnp.arange(SPECTRA, dtype=jnp.int32) % SPECTRA
    angles = product.astype(F32) * (TWO_PI / SPECTRA)
    factor = 1.0 / math.sqrt(SPECTRA)
    table = jnp.stack([jnp.cos(angles) * factor, -jnp.sin(angles) * factor], axis=1)
    weight = jnp.where(ks == 32, 1.0, 2.0)[:, None, :, None]
    table = table.astype(BF16)
    return table.reshape(64, SPECTRA), (table * weight.astype(BF16)).reshape(4, 16, SPECTRA)


def channelize_kernel(v_ref, h_ref, w_ref, t_ref, o_ref, x_ref):
    @pl.when(pl.program_id(0) == 0)
    def _():
        for s in range(4):
            total = None
            for tap in range(TAPS):
                at = s + tap - 3
                if at < 0:
                    frame = h_ref[:, (at + 3) * NFFT : (at + 4) * NFFT].astype(F32)
                else:
                    frame = v_ref[:, at * NFFT : (at + 1) * NFFT].astype(F32)
                term = w_ref[tap : tap + 1, :] * frame
                total = term if total is None else total + term
            low, high = total[:, :HALF], total[:, HALF:]
            x_ref[0, s * 64 : (s + 1) * 64, :] = (low + high).astype(BF16)
            x_ref[1, s * 64 : (s + 1) * 64, :] = (low - high).astype(BF16)

    parity = pl.program_id(0) // 4
    acc = lax.dot_general(t_ref[...], x_ref[parity], NT, preferred_element_type=F32)
    first = acc[:, :128].reshape(32, 8, 128)
    second = acc[:, 128:].reshape(32, 8, 128)
    upper = iota((32, 8, 128), 1) < 4
    even = jnp.where(upper, first, pltpu.roll(second, 4, 1))
    odd = jnp.where(upper, pltpu.roll(first, 4, 1), second)
    o_ref[:, 0] = even.astype(BF16)
    o_ref[:, 1] = odd.astype(BF16)


def channelize(voltages, halo, window, table):
    out = pl.pallas_call(
        channelize_kernel,
        grid=(8,),
        in_specs=[
            pl.BlockSpec((64, 4 * NFFT), lambda i: (0, 0)),
            pl.BlockSpec((64, 3 * NFFT), lambda i: (0, 0)),
            pl.BlockSpec((TAPS, NFFT), lambda i: (0, 0)),
            pl.BlockSpec((256, HALF), lambda i: (i, 0)),
        ],
        out_specs=pl.BlockSpec((32, 2, 8, 128), lambda i: (i, 0, 0, 0)),
        out_shape=jax.ShapeDtypeStruct((256, 2, 8, 128), BF16),
        scratch_shapes=[pltpu.VMEM((2, 256, HALF), BF16)],
        name="channelize",
    )(voltages, halo, window, table.reshape(2048, HALF))
    return out.reshape(512, 8, 128)


def beam_kernel(r_ref, slot_ref, ns_ref, ew_ref, time_ref, o_ref, z_ref, x_ref, y_ref):
    left = iota((128, 128), 1) < 64

    def assemble(g, _):
        first = r_ref[:, 2 * g].astype(F32).reshape(128, 128)
        second = r_ref[:, 2 * g + 1].astype(F32).reshape(128, 128)
        lanes = pl.ds(pl.multiple_of(g * 128, 128), 128)
        z_ref[0:128, lanes] = jnp.where(left, first, pltpu.roll(second, 64, 1)).astype(BF16)
        z_ref[128:256, lanes] = jnp.where(left, pltpu.roll(first, 64, 1), second).astype(BF16)
        return 0

    lax.fori_loop(0, 16, assemble, 0)
    row = iota((256, 256), 0)
    time = row % 64
    source = (time % 2) * 128 + (time // 4) * 8 + ((time // 2) % 2) * 4 + row // 64
    order = jnp.where(source == iota((256, 256), 1), 1.0, 0.0).astype(BF16)
    x_ref[...] = jnp.dot(order, z_ref[...], preferred_element_type=F32).astype(BF16)

    def north(cp, _):
        slots = slot_ref[pl.ds(cp, 1), :]
        select = jnp.where(iota((2048, 256), 0) == slots, 1.0, 0.0).astype(BF16)
        grid = jnp.dot(x_ref[...], select, preferred_element_type=F32).astype(BF16)
        for c in range(2):
            both = jnp.dot(grid[c * 128 : (c + 1) * 128], ns_ref[c], preferred_element_type=F32)
            y_ref[c, cp, 0] = both[:64, :256] - both[64:, 256:]
            y_ref[c, cp, 1] = both[64:, :256] + both[:64, 256:]
        return 0

    lax.fori_loop(0, 8, north, 0)
    for c in range(2):

        def east(e, _):
            power = None
            for pol in range(2):
                real, imag = None, None
                for cyl in range(4):
                    w_re = ew_ref[0, c * 16 + e * 4 + cyl]
                    w_im = ew_ref[1, c * 16 + e * 4 + cyl]
                    y_re = y_ref[c, 2 * cyl + pol, 0]
                    y_im = y_ref[c, 2 * cyl + pol, 1]
                    re = w_re * y_re - w_im * y_im
                    im = w_re * y_im + w_im * y_re
                    real = re if real is None else real + re
                    imag = im if imag is None else imag + im
                part = real * real + imag * imag
                power = part if power is None else power + part
            freq = jnp.dot(time_ref[...], power.astype(BF16), preferred_element_type=F32)
            o_ref[c, e] = freq.astype(BF16)
            return 0

        lax.fori_loop(0, 4, east, 0)


def form_beams(received, slots, ns_table, ew_table, time_table):
    vmem = pl.BlockSpec(memory_space=pltpu.VMEM)
    return pl.pallas_call(
        beam_kernel,
        in_specs=[vmem, vmem, vmem, pl.BlockSpec(memory_space=pltpu.SMEM), vmem],
        out_specs=vmem,
        out_shape=jax.ShapeDtypeStruct((2, 4, 64, 256), BF16),
        scratch_shapes=[
            pltpu.VMEM((256, 2048), BF16),
            pltpu.VMEM((256, 2048), BF16),
            pltpu.VMEM((2, 8, 2, 64, 256), F32),
        ],
        compiler_params=pltpu.CompilerParams(vmem_limit_bytes=48 << 20),
        name="beams",
    )(received, slots, ns_table, ew_table, time_table)


def search_kernel(num_ref, f_ref, d_ref, lut_ref, o_ref, ft_ref):
    @pl.when(pl.program_id(0) == 0)
    def _():
        ft_ref[...] = f_ref[...].astype(F32).T.astype(BF16)

    first_k = num_ref[0]
    last = num_ref[1]
    plain = last.astype(F32)
    scale = 1.0 - plain
    sums = [None, None]
    for parity in range(2):
        delays = d_ref[pl.ds(parity, 512, stride=2), :]
        turn = (first_k * delays) % SPECTRA
        cos = jnp.take_along_axis(jnp.broadcast_to(lut_ref[0:1, :], (512, 128)), turn, axis=1)
        sin = jnp.take_along_axis(jnp.broadcast_to(lut_ref[1:2, :], (512, 128)), turn, axis=1)
        sign = (1 - 2 * (delays % 2)).astype(F32)
        tables = (
            jnp.concatenate([cos.astype(BF16), sin.astype(BF16)], axis=1),
            jnp.concatenate(
                [(sign * (plain + scale * cos)).astype(BF16), (-scale * sign * sin).astype(BF16)], axis=1
            ),
        )
        for pair in range(2):
            part = jnp.dot(
                ft_ref[pair * 64 : (pair + 1) * 64, parity * 512 : (parity + 1) * 512],
                tables[pair],
                preferred_element_type=F32,
            )
            sums[pair] = part if sums[pair] is None else sums[pair] + part
    moved = []
    for pair in range(2):
        both = sums[pair]
        moved.append(both[:32, :128] - both[32:, 128:])
        moved.append(both[:32, 128:] + both[32:, :128])
    moved = jnp.concatenate(moved, axis=0) * (1.0 / math.sqrt(CHANS))
    o_ref[...] = moved.T.astype(BF16)


def search(numbers, freq, delays, lut):
    return pl.pallas_call(
        search_kernel,
        grid=(4,),
        in_specs=[
            pl.BlockSpec(memory_space=pltpu.SMEM),
            pl.BlockSpec((CHANS, 128), lambda i: (0, 0)),
            pl.BlockSpec((CHANS, 128), lambda i: (0, i)),
            pl.BlockSpec((8, 128), lambda i: (0, 0)),
        ],
        out_specs=pl.BlockSpec((128, 128), lambda i: (i, 0)),
        out_shape=jax.ShapeDtypeStruct((512, 128), BF16),
        scratch_shapes=[pltpu.VMEM((128, CHANS), BF16)],
        name="search",
    )(numbers, freq, delays, lut)


def local(voltages, feed_at_grid_slot, ew_grid, ns_grid, delays):
    tm = lax.axis_index("tm")
    me = tm * 32 + lax.axis_index("feed")
    everyone = ("tm", "feed")
    tail = voltages[:, NFFT:].astype(BF16)
    halo = lax.ppermute(tail, "tm", [(i, i + 1) for i in range(15)])
    window = pfb_window() * (1.0 / 64.0)
    spectra = channelize(voltages, halo, window, twiddle_tables())
    received = lax.all_to_all(spectra, everyone, split_axis=0, concat_axis=0, tiled=True)

    chan_ids = (me % 256) * 4 + me // 256 + 2 * jnp.arange(2, dtype=jnp.int32) + CHANS
    ew = steer_seed(jnp.arange(4, dtype=jnp.int32), ew_grid, chan_ids, 0.5)
    ew = jnp.stack([x.astype(BF16).astype(F32).transpose(0, 2, 1).reshape(32) for x in ew])
    slots = feed_at_grid_slot.reshape(ROWS, 8).T
    forward, backward = time_rows()
    freq = form_beams(
        received.reshape(16, 32, 8, 128), slots, north_tables(ns_grid, chan_ids), ew, forward
    )
    freq = freq.reshape(2, 4, 4, 16, 8, 32).transpose(3, 1, 4, 0, 2, 5).reshape(512, 2, 128)
    by_freq = lax.all_to_all(freq, everyone, split_axis=0, concat_axis=0, tiled=True)

    angles = jnp.arange(128, dtype=jnp.int32) % SPECTRA
    angles = angles.astype(F32) * (TWO_PI / SPECTRA)
    lut = jnp.stack([jnp.cos(angles), jnp.sin(angles)] + [jnp.zeros_like(angles)] * 6)
    numbers = jnp.stack([tm + 1, jnp.where(tm == 15, 1, 0)]).astype(jnp.int32)
    moved = search(numbers, by_freq.reshape(CHANS, 128), delays, lut)
    combined = lax.all_to_all(moved.reshape(16, 32, 128), "tm", split_axis=0, concat_axis=0, tiled=True)
    combined = combined.reshape(16, 32, 4, 32)
    return jnp.einsum("gdqb,qgt->dbt", combined, backward, preferred_element_type=F32)


def solution(mesh):
    in_specs = (P("feed", "tm"), P(), P(), P(), P())
    out_specs = P("tm", "feed", None)
    return jax.shard_map(local, mesh=mesh, in_specs=in_specs, out_specs=out_specs, check_vma=False)
```

```python
import math
from functools import partial

import jax
import jax.numpy as jnp
from jax import lax
from jax.experimental import pallas as pl
from jax.experimental.pallas import tpu as pltpu
from jax.sharding import PartitionSpec as P

NFFT = 2048
CHANS = 1024
TAPS = 4
ROWS = 256
SPECTRA = 64
HALF = NFFT // 2
TWO_PI = 2.0 * math.pi
PHASE_MODULUS = 1048576
F32 = jnp.float32
BF16 = jnp.bfloat16
NT = (((1,), (1,)), ((), ()))


VMEM = pl.BlockSpec(memory_space=pltpu.VMEM)
SMEM = pl.BlockSpec(memory_space=pltpu.SMEM)
LEAN = pltpu.CompilerParams(vmem_limit_bytes=24 << 20)


def iota(shape, axis):
    return lax.broadcasted_iota(jnp.int32, shape, axis)


def pfb_window():
    points = jnp.arange(TAPS * NFFT, dtype=F32) + 0.5
    start_offset = points / NFFT - TAPS / 2.0
    taper = 0.5 - 0.5 * jnp.cos(TWO_PI * points / (TAPS * NFFT))
    values = (jnp.sinc(start_offset) * taper).reshape(TAPS, NFFT)
    return values / jnp.sqrt(jnp.sum(values * values, axis=0, keepdims=True))


def twiddle_tables():
    coarse = iota((32, HALF), 0) * iota((32, HALF), 1) % 64
    coarse = coarse.astype(F32) * (TWO_PI / 64)
    shape = (2, 32, HALF)
    row = iota(shape, 1)
    chan = (row // 2) * 2 + iota(shape, 0)
    fine = (chan * iota(shape, 2) + (row % 2) * 512) % NFFT
    fine = fine.astype(F32) * (TWO_PI / NFFT)
    factor = 1.0 / math.sqrt(NFFT)
    seeds = (jnp.cos(coarse), jnp.sin(coarse), jnp.cos(fine) * factor, jnp.sin(fine) * factor)
    cos_a, sin_a, cos_b, sin_b = lax.optimization_barrier(seeds)
    table = cos_a[None, :, None, :] * cos_b[:, None] - sin_a[None, :, None, :] * sin_b[:, None]
    return table.astype(BF16).reshape(2, 1024, HALF)


def steer_seed(steps, grid_ids, chan_ids, factor):
    phases = steps[None, :, None] * grid_ids[None, None, :] * chan_ids[:, None, None] % PHASE_MODULUS
    angles = phases.astype(F32) * (TWO_PI / PHASE_MODULUS)
    return jnp.cos(angles) * factor, jnp.sin(angles) * factor


def north_tables(ns_grid, chan_ids):
    steps = jnp.arange(16, dtype=jnp.int32)
    seeds = steer_seed(steps * 16, ns_grid, chan_ids, 1.0) + steer_seed(steps, ns_grid, chan_ids, 1.0 / math.sqrt(ROWS))
    cos_a, sin_a, cos_b, sin_b = lax.optimization_barrier(seeds)
    cos_a, sin_a = cos_a[:, :, None, :], sin_a[:, :, None, :]
    cos_b, sin_b = cos_b[:, None], sin_b[:, None]
    real = (cos_a * cos_b - sin_a * sin_b).astype(BF16).reshape(2, ROWS, 256)
    imag = (sin_a * cos_b + cos_a * sin_b).astype(BF16).reshape(2, ROWS, 256)
    return jnp.concatenate([real, imag], axis=2)


def time_rows():
    block = jnp.arange(16, dtype=jnp.int32)
    ks = jnp.stack([block + 1, jnp.where(block == 15, 32, 31 - block)])
    product = ks[:, :, None] * jnp.arange(SPECTRA, dtype=jnp.int32) % SPECTRA
    angles = product.astype(F32) * (TWO_PI / SPECTRA)
    factor = 1.0 / math.sqrt(SPECTRA)
    table = jnp.stack([jnp.cos(angles) * factor, -jnp.sin(angles) * factor], axis=1)
    weight = jnp.where(ks == 32, 1.0, 2.0)[:, None, :, None]
    table = table.astype(BF16)
    return table.reshape(64, SPECTRA), (table * weight.astype(BF16)).reshape(4, 16, SPECTRA)


def prefilter_kernel(v_ref, w_ref, o_ref):
    for s in range(4):
        total = None
        for at in range(s + 1):
            frame = v_ref[:, at * NFFT : (at + 1) * NFFT].astype(F32)
            tap = at - s + 3
            term = w_ref[tap : tap + 1, :] * frame
            total = term if total is None else total + term
        o_ref[s] = total


def prefilter(voltages, window):
    return pl.pallas_call(
        prefilter_kernel,
        in_specs=[VMEM, VMEM],
        out_specs=VMEM,
        out_shape=jax.ShapeDtypeStruct((4, 64, NFFT), F32),
        compiler_params=LEAN,
        name="prefilter",
    )(voltages, window)


def channelize_kernel(p_ref, h_ref, w_ref, t_ref, o_ref, x_ref):
    for s in range(4):
        total = p_ref[s]
        for at in range(s - 3, 0):
            tap = at - s + 3
            total = total + w_ref[tap : tap + 1, :] * h_ref[:, (at + 3) * NFFT : (at + 4) * NFFT].astype(F32)
        low, high = total[:, :HALF], total[:, HALF:]
        x_ref[0, s * 64 : (s + 1) * 64, :] = (low + high).astype(BF16)
        x_ref[1, s * 64 : (s + 1) * 64, :] = (low - high).astype(BF16)

    upper = iota((32, 8, 128), 1) < 4

    def transform(i, _):
        acc = lax.dot_general(t_ref[i], x_ref[i // 4], NT, preferred_element_type=F32)
        first = acc[:, :128].reshape(32, 8, 128)
        second = acc[:, 128:].reshape(32, 8, 128)
        at = pl.ds(pl.multiple_of(i * 32, 32), 32)
        o_ref[at, 0] = jnp.where(upper, first, pltpu.roll(second, 4, 1)).astype(BF16)
        o_ref[at, 1] = jnp.where(upper, pltpu.roll(first, 4, 1), second).astype(BF16)
        return 0

    lax.fori_loop(0, 8, transform, 0)


def channelize(partial_sums, halo, window, table):
    out = pl.pallas_call(
        channelize_kernel,
        in_specs=[VMEM] * 4,
        out_specs=VMEM,
        out_shape=jax.ShapeDtypeStruct((256, 2, 8, 128), BF16),
        scratch_shapes=[pltpu.VMEM((2, 256, HALF), BF16)],
        compiler_params=LEAN,
        name="channelize",
    )(partial_sums, halo, window, table.reshape(8, 256, HALF))
    return out.reshape(512, 8, 128)


def select_kernel(slot_ref, o_ref):
    slots = slot_ref[pl.ds(pl.program_id(0), 1), :]

    def rows(j, _):
        at = pl.ds(pl.multiple_of(j * 256, 256), 256)
        feed = iota((256, 256), 0) + j * 256
        o_ref[0, at, :] = jnp.where(feed == slots, 1.0, 0.0).astype(BF16)
        return 0

    lax.fori_loop(0, 8, rows, 0)


def selection(slots):
    return pl.pallas_call(
        select_kernel,
        grid=(8,),
        in_specs=[VMEM],
        out_specs=pl.BlockSpec((1, 2048, 256), lambda i: (i, 0, 0)),
        out_shape=pltpu.HBM((8, 2048, 256), BF16),
        compiler_params=LEAN,
        name="selection",
    )(slots)


def beam_kernel(r_ref, select_ref, ns_ref, ew_ref, time_ref, o_ref, x_ref, y_ref, z_ref, s_ref):
    @pl.when(pl.program_id(0) == 0)
    def _():
        left = iota((128, 128), 1) < 64

        def assemble(g, _):
            first = r_ref[:, 2 * g].astype(F32).reshape(128, 128)
            second = r_ref[:, 2 * g + 1].astype(F32).reshape(128, 128)
            lanes = pl.ds(pl.multiple_of(g * 128, 128), 128)
            z_ref[0:128, lanes] = jnp.where(left, first, pltpu.roll(second, 64, 1)).astype(BF16)
            z_ref[128:256, lanes] = jnp.where(left, pltpu.roll(first, 64, 1), second).astype(BF16)
            return 0

        lax.fori_loop(0, 16, assemble, 0)
        row = iota((256, 256), 0)
        time = row % 64
        source = (time % 2) * 128 + (time // 4) * 8 + ((time // 2) % 2) * 4 + row // 64
        order = jnp.where(source == iota((256, 256), 1), 1.0, 0.0).astype(BF16)
        x_ref[...] = jnp.dot(order, z_ref[...], preferred_element_type=F32).astype(BF16)

    cp = pl.program_id(0)
    grid = jnp.dot(x_ref[...], select_ref[0], preferred_element_type=F32).astype(BF16)
    for c in range(2):
        both = jnp.dot(grid[c * 128 : (c + 1) * 128], ns_ref[c], preferred_element_type=F32)
        y_ref[c, cp, 0] = both[:64, :256] - both[64:, 256:]
        y_ref[c, cp, 1] = both[64:, :256] + both[:64, 256:]

    @pl.when(pl.program_id(0) == 7)
    def _():
        quarter = iota((16, 128), 1) // 32
        for c in range(2):

            def east(e, _):
                power = None
                for pol in range(2):
                    real, imag = None, None
                    for cyl in range(4):
                        w_re = ew_ref[0, c * 16 + e * 4 + cyl]
                        w_im = ew_ref[1, c * 16 + e * 4 + cyl]
                        y_re = y_ref[c, 2 * cyl + pol, 0]
                        y_im = y_ref[c, 2 * cyl + pol, 1]
                        re = w_re * y_re - w_im * y_im
                        im = w_re * y_im + w_im * y_re
                        real = re if real is None else real + re
                        imag = im if imag is None else imag + im
                    part = real * real + imag * imag
                    power = part if power is None else power + part
                freq = jnp.dot(time_ref[...], power.astype(BF16), preferred_element_type=F32)
                freq = freq.reshape(4, 16, 256)
                for half in range(2):
                    part = freq[:, :, half * 128 : (half + 1) * 128]
                    turned = [part] + [pltpu.roll(part, 32 * n, 2) for n in range(1, 4)]
                    for low in range(4):
                        rows = turned[-low % 4][0]
                        for q in range(1, 4):
                            rows = jnp.where(quarter == q, turned[(q - low) % 4][q], rows)
                        s_ref[pl.ds(e * 16 + (half * 4 + low) * 2 + c, 16, stride=64), :] = rows
                return 0

            lax.fori_loop(0, 4, east, 0)
        o_ref[...] = s_ref[...].astype(BF16)


def form_beams(received, select, ns_table, ew_table, time_table):
    return pl.pallas_call(
        beam_kernel,
        grid=(8,),
        in_specs=[VMEM, pl.BlockSpec((1, 2048, 256), lambda i: (i, 0, 0)), VMEM, SMEM, VMEM],
        out_specs=VMEM,
        out_shape=jax.ShapeDtypeStruct((1024, 128), BF16),
        scratch_shapes=[
            pltpu.VMEM((256, 2048), BF16),
            pltpu.VMEM((2, 8, 2, 64, 256), F32),
            pltpu.VMEM((256, 2048), BF16),
            pltpu.VMEM((1024, 128), F32),
        ],
        compiler_params=LEAN,
        name="beams",
    )(received, select, ns_table, ew_table, time_table)


def phase_kernel(num_ref, d_ref, lut_ref, o_ref):
    first_k = num_ref[0]
    plain = num_ref[1].astype(F32)
    scale = 1.0 - plain
    cos_lut = jnp.broadcast_to(lut_ref[0:1, :], (64, 128))
    sin_lut = jnp.broadcast_to(lut_ref[1:2, :], (64, 128))
    for parity in range(2):

        def fill(i, _):
            at = pl.ds(pl.multiple_of(parity * 512 + i * 64, 64), 64)
            delays = d_ref[pl.ds(i * 128 + parity, 64, stride=2), :]
            turn = (first_k * delays) & (SPECTRA - 1)
            cos = jnp.take_along_axis(cos_lut, turn, axis=1)
            sin = jnp.take_along_axis(sin_lut, turn, axis=1)
            sign = (1 - 2 * (delays & 1)).astype(F32)
            o_ref[0, at, :128] = cos.astype(BF16)
            o_ref[0, at, 128:] = sin.astype(BF16)
            o_ref[1, at, :128] = (sign * (plain + scale * cos)).astype(BF16)
            o_ref[1, at, 128:] = (-scale * sign * sin).astype(BF16)
            return 0

        lax.fori_loop(0, 8, fill, 0)


def phase_tables(numbers, delays, lut):
    return pl.pallas_call(
        phase_kernel,
        grid=(4,),
        in_specs=[SMEM, pl.BlockSpec((CHANS, 128), lambda i: (0, i)), pl.BlockSpec((8, 128), lambda i: (0, 0))],
        out_specs=pl.BlockSpec((2, CHANS, 256), lambda i: (0, 0, i)),
        out_shape=pltpu.HBM((2, CHANS, 1024), BF16),
        compiler_params=LEAN,
        name="phases",
    )(numbers, delays, lut)


def search_kernel(f_ref, t_ref, o_ref, ft_ref):
    @pl.when(pl.program_id(0) == 0)
    def _():
        ft_ref[...] = f_ref[...].astype(F32).T.astype(BF16)

    moved = []
    for pair in range(2):
        both = jnp.dot(ft_ref[pair * 64 : (pair + 1) * 64], t_ref[pair], preferred_element_type=F32)
        moved.append(both[:32, :128] - both[32:, 128:])
        moved.append(both[:32, 128:] + both[32:, :128])
    moved = jnp.concatenate(moved, axis=0) * (1.0 / math.sqrt(CHANS))
    o_ref[...] = moved.T.astype(BF16)


def search(freq, tables):
    return pl.pallas_call(
        search_kernel,
        grid=(4,),
        in_specs=[VMEM, pl.BlockSpec((2, CHANS, 256), lambda i: (0, 0, i))],
        out_specs=pl.BlockSpec((128, 128), lambda i: (i, 0)),
        out_shape=jax.ShapeDtypeStruct((512, 128), BF16),
        scratch_shapes=[pltpu.VMEM((128, CHANS), BF16)],
        compiler_params=LEAN,
        name="search",
    )(freq, tables)


def local(voltages, feed_at_grid_slot, ew_grid, ns_grid, delays):
    tm = lax.axis_index("tm")
    me = tm * 32 + lax.axis_index("feed")
    everyone = ("tm", "feed")
    tail = voltages[:, NFFT:].astype(BF16)
    halo = lax.ppermute(tail, "tm", [(i, i + 1) for i in range(15)])
    window = pfb_window() * (1.0 / 64.0)
    spectra = channelize(prefilter(voltages, window), halo, window, twiddle_tables())
    received = lax.all_to_all(spectra, everyone, split_axis=0, concat_axis=0, tiled=True)

    chan_ids = (me % 256) * 4 + me // 256 + 2 * jnp.arange(2, dtype=jnp.int32) + CHANS
    ew = steer_seed(jnp.arange(4, dtype=jnp.int32), ew_grid, chan_ids, 0.5)
    ew = jnp.stack([x.astype(BF16).astype(F32).transpose(0, 2, 1).reshape(32) for x in ew])
    slots = feed_at_grid_slot.reshape(ROWS, 8).T
    forward, backward = time_rows()
    angles = jnp.arange(128, dtype=jnp.int32) % SPECTRA
    angles = angles.astype(F32) * (TWO_PI / SPECTRA)
    lut = jnp.stack([jnp.cos(angles), jnp.sin(angles)] + [jnp.zeros_like(angles)] * 6)
    numbers = jnp.stack([tm + 1, jnp.where(tm == 15, 1, 0)]).astype(jnp.int32)
    tables = phase_tables(numbers, delays, lut)
    received, tables = lax.optimization_barrier((received, tables))
    tables = pltpu.with_memory_space_constraint(tables, pltpu.HBM)
    select = pltpu.with_memory_space_constraint(selection(slots), pltpu.HBM)
    freq = form_beams(
        received.reshape(16, 32, 8, 128), select, north_tables(ns_grid, chan_ids), ew, forward
    )
    by_freq = lax.all_to_all(freq.reshape(512, 2, 128), everyone, split_axis=0, concat_axis=0, tiled=True)
    moved = search(by_freq.reshape(CHANS, 128), tables)
    combined = lax.all_to_all(moved.reshape(16, 32, 128), "tm", split_axis=0, concat_axis=0, tiled=True)
    combined = combined.reshape(16, 32, 4, 32)
    return jnp.einsum("gdqb,qgt->dbt", combined, backward, preferred_element_type=F32)


def solution(mesh):
    in_specs = (P("feed", "tm"), P(), P(), P(), P())
    out_specs = P("tm", "feed", None)
    return jax.shard_map(local, mesh=mesh, in_specs=in_specs, out_specs=out_specs, check_vma=False)
```

```python
import math
from functools import partial

import jax
import jax.numpy as jnp
from jax import lax
from jax.experimental import pallas as pl
from jax.experimental.pallas import tpu as pltpu
from jax.sharding import Mesh, PartitionSpec as P

NFFT = 2048
CHANS = 1024
TAPS = 4
ROWS = 256
SPECTRA = 64
HALF = NFFT // 2
TWO_PI = 2.0 * math.pi
PHASE_MODULUS = 1048576
F32 = jnp.float32
TIME = ("y", "z_lo")
FEED = ("z_hi", "x", "core")
BF16 = jnp.bfloat16
NT = (((1,), (1,)), ((), ()))


VMEM = pl.BlockSpec(memory_space=pltpu.VMEM)
SMEM = pl.BlockSpec(memory_space=pltpu.SMEM)
LEAN = pltpu.CompilerParams(vmem_limit_bytes=24 << 20)


def iota(shape, axis):
    return lax.broadcasted_iota(jnp.int32, shape, axis)


def pfb_window():
    points = jnp.arange(TAPS * NFFT, dtype=F32) + 0.5
    start_offset = points / NFFT - TAPS / 2.0
    taper = 0.5 - 0.5 * jnp.cos(TWO_PI * points / (TAPS * NFFT))
    values = (jnp.sinc(start_offset) * taper).reshape(TAPS, NFFT)
    return values / jnp.sqrt(jnp.sum(values * values, axis=0, keepdims=True))


def twiddle_tables():
    coarse = iota((32, HALF), 0) * iota((32, HALF), 1) % 64
    coarse = coarse.astype(F32) * (TWO_PI / 64)
    shape = (2, 32, HALF)
    row = iota(shape, 1)
    chan = (row // 2) * 2 + iota(shape, 0)
    fine = (chan * iota(shape, 2) + (row % 2) * 512) % NFFT
    fine = fine.astype(F32) * (TWO_PI / NFFT)
    factor = 1.0 / math.sqrt(NFFT)
    seeds = (jnp.cos(coarse), jnp.sin(coarse), jnp.cos(fine) * factor, jnp.sin(fine) * factor)
    cos_a, sin_a, cos_b, sin_b = lax.optimization_barrier(seeds)
    table = cos_a[None, :, None, :] * cos_b[:, None] - sin_a[None, :, None, :] * sin_b[:, None]
    return table.astype(BF16).reshape(2, 1024, HALF)


def steer_seed(steps, grid_ids, chan_ids, factor):
    phases = steps[None, :, None] * grid_ids[None, None, :] * chan_ids[:, None, None] % PHASE_MODULUS
    angles = phases.astype(F32) * (TWO_PI / PHASE_MODULUS)
    return jnp.cos(angles) * factor, jnp.sin(angles) * factor


def north_tables(ns_grid, chan_ids):
    steps = jnp.arange(16, dtype=jnp.int32)
    seeds = steer_seed(steps * 16, ns_grid, chan_ids, 1.0) + steer_seed(steps, ns_grid, chan_ids, 1.0 / math.sqrt(ROWS))
    cos_a, sin_a, cos_b, sin_b = lax.optimization_barrier(seeds)
    cos_a, sin_a = cos_a[:, :, None, :], sin_a[:, :, None, :]
    cos_b, sin_b = cos_b[:, None], sin_b[:, None]
    real = (cos_a * cos_b - sin_a * sin_b).astype(BF16).reshape(2, ROWS, 256)
    imag = (sin_a * cos_b + cos_a * sin_b).astype(BF16).reshape(2, ROWS, 256)
    return jnp.concatenate([real, imag], axis=2)


def time_rows():
    block = jnp.arange(16, dtype=jnp.int32)
    ks = jnp.stack([block + 1, jnp.where(block == 15, 32, 31 - block)])
    product = ks[:, :, None] * jnp.arange(SPECTRA, dtype=jnp.int32) % SPECTRA
    angles = product.astype(F32) * (TWO_PI / SPECTRA)
    factor = 1.0 / math.sqrt(SPECTRA)
    table = jnp.stack([jnp.cos(angles) * factor, -jnp.sin(angles) * factor], axis=1)
    weight = jnp.where(ks == 32, 1.0, 2.0)[:, None, :, None]
    table = table.astype(BF16)
    return jnp.roll(table, -1, axis=-1).reshape(64, SPECTRA), (table * weight.astype(BF16)).reshape(4, 16, SPECTRA)


def prefilter_kernel(keep_ref, v_ref, w_ref, o_ref):
    for s in range(1, 5):
        total = None
        for at in range(max(0, s - 3), min(4, s + 1)):
            frame = v_ref[:, at * NFFT : (at + 1) * NFFT].astype(F32)
            tap = at - s + 3
            term = w_ref[tap : tap + 1, :] * frame
            total = term if total is None else total + term
        o_ref[s - 1] = total if s < 4 else jnp.where(keep_ref[0] == 1, total, 0.0)


def in_hbm(x):
    return pltpu.with_memory_space_constraint(x, pltpu.HBM)


def whole(shape):
    return pl.BlockSpec(shape, lambda i: (0, 0))


def edges_kernel(v_ref, back_ref, ahead_ref):
    frame = v_ref[...].astype(BF16)

    @pl.when(pl.program_id(0) < 2)
    def _():
        back_ref[...] = frame

    @pl.when(pl.program_id(0) == 2)
    def _():
        ahead_ref[...] = frame


def edges(voltages):
    return pl.pallas_call(
        edges_kernel,
        grid=(3,),
        in_specs=[pl.BlockSpec((64, NFFT), lambda i: (0, (i + 2) % 4))],
        out_specs=[pl.BlockSpec((64, NFFT), lambda i: (0, jnp.minimum(i, 1))), whole((64, NFFT))],
        out_shape=[jax.ShapeDtypeStruct((64, 2 * NFFT), BF16), jax.ShapeDtypeStruct((64, NFFT), BF16)],
        compiler_params=LEAN,
        name="edges",
    )(voltages)


def prefilter(keep, voltages, window):
    return pl.pallas_call(
        prefilter_kernel,
        in_specs=[SMEM, VMEM, VMEM],
        out_specs=VMEM,
        out_shape=jax.ShapeDtypeStruct((4, 64, NFFT), F32),
        compiler_params=LEAN,
        name="prefilter",
    )(keep, voltages, window)


def channelize_kernel(p_ref, back_ref, ahead_ref, w_ref, t_ref, o_ref, x_ref):
    @pl.when(pl.program_id(0) == 0)
    def _():
        def filter_rows(i, _):
            at = pl.ds(pl.multiple_of(i * 16, 16), 16)

            def term(tap, ref, frame):
                return w_ref[tap : tap + 1, :] * ref[at, frame * NFFT : (frame + 1) * NFFT].astype(F32)

            for s in range(4):
                total = p_ref[s, at, :]
                if s == 0:
                    total = total + term(0, back_ref, 0) + term(1, back_ref, 1)
                elif s == 1:
                    total = total + term(0, back_ref, 1)
                elif s == 3:
                    total = total + term(3, ahead_ref, 0)
                low, high = total[:, :HALF], total[:, HALF:]
                to = pl.ds(pl.multiple_of(s * 64 + i * 16, 16), 16)
                x_ref[0, to, :] = (low + high).astype(BF16)
                x_ref[1, to, :] = (low - high).astype(BF16)
            return 0

        lax.fori_loop(0, 4, filter_rows, 0)

    upper = iota((64, 8, 128), 1) < 4
    acc = lax.dot_general(t_ref[...], x_ref[pl.program_id(0) // 2], NT, preferred_element_type=F32)
    first = acc[:, :128].reshape(64, 8, 128)
    second = acc[:, 128:].reshape(64, 8, 128)
    o_ref[:, 0] = jnp.where(upper, first, pltpu.roll(second, 4, 1)).astype(BF16)
    o_ref[:, 1] = jnp.where(upper, pltpu.roll(first, 4, 1), second).astype(BF16)


def channelize(partial_sums, back, ahead, window, table):
    out = pl.pallas_call(
        channelize_kernel,
        grid=(4,),
        in_specs=[VMEM, whole((64, 2 * NFFT)), whole((64, NFFT)), VMEM]
        + [pl.BlockSpec((512, HALF), lambda i: (i, 0))],
        out_specs=pl.BlockSpec((64, 2, 8, 128), lambda i: (i, 0, 0, 0)),
        out_shape=jax.ShapeDtypeStruct((256, 2, 8, 128), BF16),
        scratch_shapes=[pltpu.VMEM((2, 256, HALF), BF16)],
        compiler_params=LEAN,
        name="channelize",
    )(partial_sums, in_hbm(back), in_hbm(ahead), window, in_hbm(table.reshape(2048, HALF)))
    return out.reshape(512, 8, 128)


def select_kernel(slot_ref, o_ref):
    slots = slot_ref[pl.ds(pl.program_id(0), 1), :]

    def rows(j, _):
        at = pl.ds(pl.multiple_of(j * 256, 256), 256)
        feed = iota((256, 256), 0) + j * 256
        o_ref[0, at, :] = jnp.where(feed == slots, 1.0, 0.0).astype(BF16)
        return 0

    lax.fori_loop(0, 8, rows, 0)


def selection(slots):
    return pl.pallas_call(
        select_kernel,
        grid=(8,),
        in_specs=[VMEM],
        out_specs=pl.BlockSpec((1, 2048, 256), lambda i: (i, 0, 0)),
        out_shape=pltpu.HBM((8, 2048, 256), BF16),
        compiler_params=LEAN,
        name="selection",
    )(slots)


def beam_kernel(r_ref, select_ref, ns_ref, ew_ref, time_ref, o_ref, x_ref, y_ref, z_ref, s_ref):
    @pl.when(pl.program_id(0) == 0)
    def _():
        left = iota((128, 128), 1) < 64

        def assemble(g, _):
            first = r_ref[0, g // 4, :, g % 4].astype(F32).reshape(128, 128)
            second = r_ref[1, g // 4, :, g % 4].astype(F32).reshape(128, 128)
            lanes = pl.ds(pl.multiple_of(g * 128, 128), 128)
            z_ref[0:128, lanes] = jnp.where(left, first, pltpu.roll(second, 64, 1)).astype(BF16)
            z_ref[128:256, lanes] = jnp.where(left, pltpu.roll(first, 64, 1), second).astype(BF16)
            return 0

        lax.fori_loop(0, 16, assemble, 0)
        row = iota((256, 256), 0)
        time = row % 64
        source = (time % 2) * 128 + ((time // 4) % 2) * 64 + (time // 8) * 8 + ((time // 2) % 2) * 4 + row // 64
        order = jnp.where(source == iota((256, 256), 1), 1.0, 0.0).astype(BF16)
        x_ref[...] = jnp.dot(order, z_ref[...], preferred_element_type=F32).astype(BF16)

    grids = [jnp.dot(x_ref[...], select_ref[pol], preferred_element_type=F32).astype(BF16) for pol in range(2)]
    cyl = pl.program_id(0)
    for c in range(2):
        rows = jnp.concatenate([grid[c * 128 : (c + 1) * 128] for grid in grids], axis=0)
        both = jnp.dot(rows, ns_ref[c], preferred_element_type=F32)
        for pol in range(2):
            y_ref[c, cyl, pol, 0] = both[pol * 128 : pol * 128 + 64, :256] - both[pol * 128 + 64 : pol * 128 + 128, 256:]
            y_ref[c, cyl, pol, 1] = both[pol * 128 + 64 : pol * 128 + 128, :256] + both[pol * 128 : pol * 128 + 64, 256:]

    @pl.when(pl.program_id(0) == 3)
    def _():
        quarter = iota((16, 128), 1) // 32
        for c in range(2):

            def east(e, _):
                power = None
                for pol in range(2):
                    real = 0.5 * y_ref[c, 0, pol, 0]
                    imag = 0.5 * y_ref[c, 0, pol, 1]
                    for cyl in range(1, 4):
                        w_re = ew_ref[0, c * 16 + e * 4 + cyl]
                        w_im = ew_ref[1, c * 16 + e * 4 + cyl]
                        y_re = y_ref[c, cyl, pol, 0]
                        y_im = y_ref[c, cyl, pol, 1]
                        real = real + (w_re * y_re - w_im * y_im)
                        imag = imag + (w_re * y_im + w_im * y_re)
                    part = real * real + imag * imag
                    power = part if power is None else power + part
                freq = jnp.dot(time_ref[...], power.astype(BF16), preferred_element_type=F32)
                freq = freq.reshape(4, 16, 256)
                for half in range(2):
                    part = freq[:, :, half * 128 : (half + 1) * 128]
                    turned = [part] + [pltpu.roll(part, 32 * n, 2) for n in range(1, 4)]
                    for low in range(4):
                        rows = turned[-low % 4][0]
                        for q in range(1, 4):
                            rows = jnp.where(quarter == q, turned[(q - low) % 4][q], rows)
                        bh = half * 4 + low
                        start = ((bh % 2) * 256 + e * 64 + bh // 2) * 2 + c
                        s_ref[pl.ds(start, 16, stride=8), :] = rows
                return 0

            lax.fori_loop(0, 4, east, 0)
        o_ref[...] = s_ref[...].astype(BF16)


def form_beams(received, select, ns_table, ew_table, time_table):
    return pl.pallas_call(
        beam_kernel,
        grid=(4,),
        in_specs=[VMEM, pl.BlockSpec((2, 2048, 256), lambda i: (i, 0, 0)), VMEM, SMEM, VMEM],
        out_specs=VMEM,
        out_shape=jax.ShapeDtypeStruct((1024, 128), BF16),
        scratch_shapes=[
            pltpu.VMEM((256, 2048), BF16),
            pltpu.VMEM((2, 4, 2, 2, 64, 256), F32),
            pltpu.VMEM((256, 2048), BF16),
            pltpu.VMEM((1024, 128), F32),
        ],
        compiler_params=LEAN,
        name="beams",
    )(received, select, ns_table, ew_table, time_table)


def phase_kernel(num_ref, d_ref, lut_ref, o_ref):
    first_k = num_ref[0]
    plain = num_ref[1].astype(F32)
    scale = 1.0 - plain
    cos_lut = jnp.broadcast_to(lut_ref[0:1, :], (64, 128))
    sin_lut = jnp.broadcast_to(lut_ref[1:2, :], (64, 128))
    for parity in range(2):

        def fill(i, _):
            at = pl.ds(pl.multiple_of(parity * 512 + i * 64, 64), 64)
            delays = d_ref[pl.ds(i * 128 + parity, 64, stride=2), :]
            turn = (first_k * delays) & (SPECTRA - 1)
            cos = jnp.take_along_axis(cos_lut, turn, axis=1)
            sin = jnp.take_along_axis(sin_lut, turn, axis=1)
            sign = (1 - 2 * (delays & 1)).astype(F32)
            o_ref[0, at, :128] = cos.astype(BF16)
            o_ref[0, at, 128:] = sin.astype(BF16)
            o_ref[1, at, :128] = (sign * (plain + scale * cos)).astype(BF16)
            o_ref[1, at, 128:] = (-scale * sign * sin).astype(BF16)
            return 0

        lax.fori_loop(0, 8, fill, 0)


def phase_tables(numbers, delays, lut):
    return pl.pallas_call(
        phase_kernel,
        grid=(4,),
        in_specs=[SMEM, pl.BlockSpec((CHANS, 128), lambda i: (0, i)), pl.BlockSpec((8, 128), lambda i: (0, 0))],
        out_specs=pl.BlockSpec((2, CHANS, 256), lambda i: (0, 0, i)),
        out_shape=pltpu.HBM((2, CHANS, 1024), BF16),
        compiler_params=LEAN,
        name="phases",
    )(numbers, delays, lut)


def search_kernel(f_ref, t_ref, o_ref):
    freq = f_ref[...].astype(F32).T.astype(BF16)
    sums = [jnp.dot(freq[pair * 64 : (pair + 1) * 64], t_ref[pair], preferred_element_type=F32) for pair in range(2)]
    for j in range(4):
        moved = []
        for pair in range(2):
            cos = sums[pair][:, j * 256 : j * 256 + 128]
            sin = sums[pair][:, j * 256 + 128 : j * 256 + 256]
            moved.append(cos[:32] - sin[32:])
            moved.append(sin[:32] + cos[32:])
        moved = jnp.concatenate(moved, axis=0) * (1.0 / math.sqrt(CHANS))
        o_ref[j * 128 : (j + 1) * 128, :] = moved.T.astype(BF16)


def search(freq, tables):
    return pl.pallas_call(
        search_kernel,
        in_specs=[VMEM, VMEM],
        out_specs=VMEM,
        out_shape=jax.ShapeDtypeStruct((512, 128), BF16),
        compiler_params=LEAN,
        name="search",
    )(freq, tables)


def local(voltages, feed_at_grid_slot, ew_grid, ns_grid, delays):
    tm = lax.axis_index(TIME)
    everyone = ("core", "z_hi", "z_lo", "y", "x")
    me = lax.axis_index(everyone)
    block = lax.axis_index(("z_lo", "y"))
    back, ahead = edges(in_hbm(voltages))
    back = lax.ppermute(back, TIME, [(i, i + 1) for i in range(15)])
    ahead = lax.ppermute(ahead, TIME, [((i + 1) % 16, i) for i in range(16)])
    window = pfb_window() * (1.0 / 64.0)
    keep = jnp.where(tm == 15, 0, 1).astype(jnp.int32).reshape(1)
    spectra = channelize(prefilter(keep, voltages, window), back, ahead, window, twiddle_tables())
    received = lax.all_to_all(spectra, everyone, split_axis=0, concat_axis=0, tiled=True)

    chan_ids = (me % 256) * 4 + me // 256 + 2 * jnp.arange(2, dtype=jnp.int32) + CHANS
    ew = steer_seed(jnp.arange(4, dtype=jnp.int32), ew_grid, chan_ids, 0.5)
    ew = jnp.stack([x.astype(BF16).astype(F32).transpose(0, 2, 1).reshape(32) for x in ew])
    slots = feed_at_grid_slot.reshape(ROWS, 8).T
    forward, backward = time_rows()
    angles = jnp.arange(128, dtype=jnp.int32) % SPECTRA
    angles = angles.astype(F32) * (TWO_PI / SPECTRA)
    lut = jnp.stack([jnp.cos(angles), jnp.sin(angles)] + [jnp.zeros_like(angles)] * 6)
    numbers = jnp.stack([block + 1, jnp.where(block == 15, 1, 0)]).astype(jnp.int32)
    tables = phase_tables(numbers, delays, lut)
    received, tables = lax.optimization_barrier((received, tables))
    select = pltpu.with_memory_space_constraint(selection(slots), pltpu.HBM)
    freq = form_beams(
        received.reshape(2, 4, 16, 4, 8, 128), select, north_tables(ns_grid, chan_ids), ew, forward
    )
    by_freq = lax.all_to_all(freq.reshape(512, 2, 128), everyone, split_axis=0, concat_axis=0, tiled=True)
    moved = search(by_freq.reshape(CHANS, 128), tables)
    combined = lax.all_to_all(moved.reshape(16, 32, 128), TIME, split_axis=0, concat_axis=0, tiled=True)
    combined = combined.reshape(16, 32, 4, 32)
    backward = backward.reshape(4, 2, 8, SPECTRA).transpose(0, 2, 1, 3).reshape(4, 16, SPECTRA)
    return jnp.einsum("gdqb,qgt->dbt", combined, backward, preferred_element_type=F32)


def solution(mesh):
    split = Mesh(mesh.devices.reshape(8, 2, 4, 4, 2), ("y", "z_lo", "z_hi", "x", "core"))
    in_specs = (P(FEED, TIME), P(), P(), P(), P())
    return jax.shard_map(local, mesh=split, in_specs=in_specs, out_specs=P(TIME, FEED, None), check_vma=False)
```

```python
import math
from functools import partial

import jax
import jax.numpy as jnp
from jax import lax
from jax.experimental import pallas as pl
from jax.experimental.pallas import tpu as pltpu
from jax.sharding import Mesh, PartitionSpec as P

NFFT = 2048
CHANS = 1024
TAPS = 4
ROWS = 256
SPECTRA = 64
HALF = NFFT // 2
TWO_PI = 2.0 * math.pi
PHASE_MODULUS = 1048576
F32 = jnp.float32
TIME = ("y", "z_lo")
FEED = ("z_hi", "x", "core")
BF16 = jnp.bfloat16
NT = (((1,), (1,)), ((), ()))


VMEM = pl.BlockSpec(memory_space=pltpu.VMEM)
SMEM = pl.BlockSpec(memory_space=pltpu.SMEM)
LEAN = pltpu.CompilerParams(vmem_limit_bytes=24 << 20)


def iota(shape, axis):
    return lax.broadcasted_iota(jnp.int32, shape, axis)


def pfb_window():
    points = jnp.arange(TAPS * NFFT, dtype=F32) + 0.5
    start_offset = points / NFFT - TAPS / 2.0
    taper = 0.5 - 0.5 * jnp.cos(TWO_PI * points / (TAPS * NFFT))
    values = (jnp.sinc(start_offset) * taper).reshape(TAPS, NFFT)
    return values / jnp.sqrt(jnp.sum(values * values, axis=0, keepdims=True))


def twiddle_tables():
    coarse = iota((32, HALF), 0) * iota((32, HALF), 1) % 64
    coarse = coarse.astype(F32) * (TWO_PI / 64)
    shape = (2, 32, HALF)
    row = iota(shape, 1)
    chan = (row // 2) * 2 + iota(shape, 0)
    fine = (chan * iota(shape, 2) + (row % 2) * 512) % NFFT
    fine = fine.astype(F32) * (TWO_PI / NFFT)
    factor = 1.0 / math.sqrt(NFFT)
    seeds = (jnp.cos(coarse), jnp.sin(coarse), jnp.cos(fine) * factor, jnp.sin(fine) * factor)
    cos_a, sin_a, cos_b, sin_b = lax.optimization_barrier(seeds)
    table = cos_a[None, :, None, :] * cos_b[:, None] - sin_a[None, :, None, :] * sin_b[:, None]
    return table.astype(BF16).reshape(2, 1024, HALF)


def steer_seed(steps, grid_ids, chan_ids, factor):
    phases = steps[None, :, None] * grid_ids[None, None, :] * chan_ids[:, None, None] % PHASE_MODULUS
    angles = phases.astype(F32) * (TWO_PI / PHASE_MODULUS)
    return jnp.cos(angles) * factor, jnp.sin(angles) * factor


def north_tables(ns_grid, chan_ids):
    steps = jnp.arange(16, dtype=jnp.int32)
    seeds = steer_seed(steps * 16, ns_grid, chan_ids, 1.0) + steer_seed(steps, ns_grid, chan_ids, 1.0 / math.sqrt(ROWS))
    cos_a, sin_a, cos_b, sin_b = lax.optimization_barrier(seeds)
    cos_a, sin_a = cos_a[:, :, None, :], sin_a[:, :, None, :]
    cos_b, sin_b = cos_b[:, None], sin_b[:, None]
    real = (cos_a * cos_b - sin_a * sin_b).astype(BF16).reshape(2, ROWS, 256)
    imag = (sin_a * cos_b + cos_a * sin_b).astype(BF16).reshape(2, ROWS, 256)
    return jnp.concatenate([real, imag], axis=2)


def time_rows():
    block = jnp.arange(16, dtype=jnp.int32)
    ks = jnp.stack([block + 1, jnp.where(block == 15, 32, 31 - block)])
    product = ks[:, :, None] * jnp.arange(SPECTRA, dtype=jnp.int32) % SPECTRA
    angles = product.astype(F32) * (TWO_PI / SPECTRA)
    factor = 1.0 / math.sqrt(SPECTRA)
    table = jnp.stack([jnp.cos(angles) * factor, -jnp.sin(angles) * factor], axis=1)
    weight = jnp.where(ks == 32, 1.0, 2.0)[:, None, :, None]
    table = table.astype(BF16)
    return jnp.roll(table, -1, axis=-1).reshape(64, SPECTRA), (table * weight.astype(BF16)).reshape(4, 16, SPECTRA)


def prefilter_kernel(keep_ref, v_ref, w_ref, o_ref):
    for s in range(1, 5):
        total = None
        for at in range(max(0, s - 3), min(4, s + 1)):
            frame = v_ref[:, at * NFFT : (at + 1) * NFFT].astype(F32)
            tap = at - s + 3
            term = w_ref[tap : tap + 1, :] * frame
            total = term if total is None else total + term
        o_ref[s - 1] = total if s < 4 else jnp.where(keep_ref[0] == 1, total, 0.0)


def in_hbm(x):
    return pltpu.with_memory_space_constraint(x, pltpu.HBM)


def whole(shape):
    return pl.BlockSpec(shape, lambda i: (0, 0))


def edges_kernel(v_ref, back_ref, ahead_ref):
    frame = v_ref[...].astype(BF16)

    @pl.when(pl.program_id(0) < 2)
    def _():
        back_ref[...] = frame

    @pl.when(pl.program_id(0) == 2)
    def _():
        ahead_ref[...] = frame


def edges(voltages):
    return pl.pallas_call(
        edges_kernel,
        grid=(3,),
        in_specs=[pl.BlockSpec((64, NFFT), lambda i: (0, (i + 2) % 4))],
        out_specs=[pl.BlockSpec((64, NFFT), lambda i: (0, jnp.minimum(i, 1))), whole((64, NFFT))],
        out_shape=[jax.ShapeDtypeStruct((64, 2 * NFFT), BF16), jax.ShapeDtypeStruct((64, NFFT), BF16)],
        compiler_params=LEAN,
        name="edges",
    )(voltages)


def prefilter(keep, voltages, window):
    return pl.pallas_call(
        prefilter_kernel,
        in_specs=[SMEM, VMEM, VMEM],
        out_specs=VMEM,
        out_shape=jax.ShapeDtypeStruct((4, 64, NFFT), F32),
        compiler_params=LEAN,
        name="prefilter",
    )(keep, voltages, window)


def channelize_kernel(p_ref, back_ref, ahead_ref, w_ref, t_ref, o_ref, x_ref):
    @pl.when(pl.program_id(0) == 0)
    def _():
        def filter_rows(i, _):
            at = pl.ds(pl.multiple_of(i * 16, 16), 16)

            def term(tap, ref, frame):
                return w_ref[tap : tap + 1, :] * ref[at, frame * NFFT : (frame + 1) * NFFT].astype(F32)

            for s in range(4):
                total = p_ref[s, at, :]
                if s == 0:
                    total = total + term(0, back_ref, 0) + term(1, back_ref, 1)
                elif s == 1:
                    total = total + term(0, back_ref, 1)
                elif s == 3:
                    total = total + term(3, ahead_ref, 0)
                low, high = total[:, :HALF], total[:, HALF:]
                to = pl.ds(pl.multiple_of(s * 64 + i * 16, 16), 16)
                x_ref[0, to, :] = (low + high).astype(BF16)
                x_ref[1, to, :] = (low - high).astype(BF16)
            return 0

        lax.fori_loop(0, 4, filter_rows, 0)

    upper = iota((64, 8, 128), 1) < 4
    acc = lax.dot_general(t_ref[...], x_ref[pl.program_id(0) // 2], NT, preferred_element_type=F32)
    first = acc[:, :128].reshape(64, 8, 128)
    second = acc[:, 128:].reshape(64, 8, 128)
    o_ref[:, 0] = jnp.where(upper, first, pltpu.roll(second, 4, 1)).astype(BF16)
    o_ref[:, 1] = jnp.where(upper, pltpu.roll(first, 4, 1), second).astype(BF16)


def channelize(partial_sums, back, ahead, window, table):
    out = pl.pallas_call(
        channelize_kernel,
        grid=(4,),
        in_specs=[VMEM, whole((64, 2 * NFFT)), whole((64, NFFT)), VMEM]
        + [pl.BlockSpec((512, HALF), lambda i: (i, 0))],
        out_specs=pl.BlockSpec((64, 2, 8, 128), lambda i: (i, 0, 0, 0)),
        out_shape=jax.ShapeDtypeStruct((256, 2, 8, 128), BF16),
        scratch_shapes=[pltpu.VMEM((2, 256, HALF), BF16)],
        compiler_params=LEAN,
        name="channelize",
    )(partial_sums, in_hbm(back), in_hbm(ahead), window, in_hbm(table.reshape(2048, HALF)))
    return out.reshape(512, 8, 128)


def select_kernel(slot_ref, o_ref):
    slots = slot_ref[pl.ds(pl.program_id(0), 1), :]

    def rows(j, _):
        at = pl.ds(pl.multiple_of(j * 256, 256), 256)
        feed = iota((256, 256), 0) + j * 256
        o_ref[0, at, :] = jnp.where(feed == slots, 1.0, 0.0).astype(BF16)
        return 0

    lax.fori_loop(0, 8, rows, 0)


def selection(slots):
    return pl.pallas_call(
        select_kernel,
        grid=(8,),
        in_specs=[VMEM],
        out_specs=pl.BlockSpec((1, 2048, 256), lambda i: (i, 0, 0)),
        out_shape=pltpu.HBM((8, 2048, 256), BF16),
        compiler_params=LEAN,
        name="selection",
    )(slots)


def beam_kernel(r_ref, select_ref, ns_ref, ew_ref, time_ref, o_ref, x_ref, y_ref, z_ref, s_ref):
    @pl.when(pl.program_id(0) == 0)
    def _():
        left = iota((128, 128), 1) < 64

        def assemble(g, _):
            first = r_ref[0, g // 4, :, g % 4].astype(F32).reshape(128, 128)
            second = r_ref[1, g // 4, :, g % 4].astype(F32).reshape(128, 128)
            lanes = pl.ds(pl.multiple_of(g * 128, 128), 128)
            z_ref[0:128, lanes] = jnp.where(left, first, pltpu.roll(second, 64, 1)).astype(BF16)
            z_ref[128:256, lanes] = jnp.where(left, pltpu.roll(first, 64, 1), second).astype(BF16)
            return 0

        lax.fori_loop(0, 16, assemble, 0)
        row = iota((256, 256), 0)
        time = row % 64
        source = (time % 2) * 128 + ((time // 4) % 2) * 64 + (time // 8) * 8 + ((time // 2) % 2) * 4 + row // 64
        order = jnp.where(source == iota((256, 256), 1), 1.0, 0.0).astype(BF16)
        x_ref[...] = jnp.dot(order, z_ref[...], preferred_element_type=F32).astype(BF16)

    grids = [jnp.dot(x_ref[...], select_ref[pol], preferred_element_type=F32).astype(BF16) for pol in range(2)]
    cyl = pl.program_id(0)
    for c in range(2):
        rows = jnp.concatenate([grid[c * 128 : (c + 1) * 128] for grid in grids], axis=0)
        both = jnp.dot(rows, ns_ref[c], preferred_element_type=F32)
        for pol in range(2):
            y_ref[c, cyl, pol, 0] = both[pol * 128 : pol * 128 + 64, :256] - both[pol * 128 + 64 : pol * 128 + 128, 256:]
            y_ref[c, cyl, pol, 1] = both[pol * 128 + 64 : pol * 128 + 128, :256] + both[pol * 128 : pol * 128 + 64, 256:]

    @pl.when(pl.program_id(0) == 3)
    def _():
        quarter = iota((16, 128), 1) // 32
        for c in range(2):

            def east_beam(e):
                power = None
                for pol in range(2):
                    real = 0.5 * y_ref[c, 0, pol, 0]
                    imag = 0.5 * y_ref[c, 0, pol, 1]
                    for cyl in range(1, 4):
                        w_re = ew_ref[0, c * 16 + e * 4 + cyl]
                        w_im = ew_ref[1, c * 16 + e * 4 + cyl]
                        y_re = y_ref[c, cyl, pol, 0]
                        y_im = y_ref[c, cyl, pol, 1]
                        real = real + (w_re * y_re - w_im * y_im)
                        imag = imag + (w_re * y_im + w_im * y_re)
                    part = real * real + imag * imag
                    power = part if power is None else power + part
                freq = jnp.dot(time_ref[...], power.astype(BF16), preferred_element_type=F32)
                freq = freq.reshape(4, 16, 256)
                for half in range(2):
                    part = freq[:, :, half * 128 : (half + 1) * 128]
                    turned = [part] + [pltpu.roll(part, 32 * n, 2) for n in range(1, 4)]
                    for low in range(4):
                        rows = turned[-low % 4][0]
                        for q in range(1, 4):
                            rows = jnp.where(quarter == q, turned[(q - low) % 4][q], rows)
                        bh = half * 4 + low
                        start = ((bh % 2) * 256 + e * 64 + bh // 2) * 2 + c
                        s_ref[pl.ds(start, 16, stride=8), :] = rows

            def east(i, _):
                east_beam(2 * i)
                east_beam(2 * i + 1)
                return 0

            lax.fori_loop(0, 2, east, 0)
        o_ref[...] = s_ref[...].astype(BF16)


def form_beams(received, select, ns_table, ew_table, time_table):
    return pl.pallas_call(
        beam_kernel,
        grid=(4,),
        in_specs=[VMEM, pl.BlockSpec((2, 2048, 256), lambda i: (i, 0, 0)), VMEM, SMEM, VMEM],
        out_specs=VMEM,
        out_shape=jax.ShapeDtypeStruct((1024, 128), BF16),
        scratch_shapes=[
            pltpu.VMEM((256, 2048), BF16),
            pltpu.VMEM((2, 4, 2, 2, 64, 256), F32),
            pltpu.VMEM((256, 2048), BF16),
            pltpu.VMEM((1024, 128), F32),
        ],
        compiler_params=LEAN,
        name="beams",
    )(received, select, ns_table, ew_table, time_table)


def phase_kernel(num_ref, d_ref, lut_ref, o_ref):
    first_k = num_ref[0]
    plain = num_ref[1].astype(F32)
    scale = 1.0 - plain
    cos_lut = jnp.broadcast_to(lut_ref[0:1, :], (256, 128))
    sin_lut = jnp.broadcast_to(lut_ref[1:2, :], (256, 128))
    for parity in range(2):

        def fill(i, _):
            at = pl.ds(pl.multiple_of(parity * 512 + i * 256, 256), 256)
            delays = d_ref[pl.ds(i * 512 + parity, 256, stride=2), :]
            turn = (first_k * delays) & (SPECTRA - 1)
            cos = jnp.take_along_axis(cos_lut, turn, axis=1)
            sin = jnp.take_along_axis(sin_lut, turn, axis=1)
            sign = (1 - 2 * (delays & 1)).astype(F32)
            o_ref[0, at, :128] = cos.astype(BF16)
            o_ref[0, at, 128:] = sin.astype(BF16)
            o_ref[1, at, :128] = (sign * (plain + scale * cos)).astype(BF16)
            o_ref[1, at, 128:] = (-scale * sign * sin).astype(BF16)
            return 0

        lax.fori_loop(0, 2, fill, 0)


def phase_tables(numbers, delays, lut):
    return pl.pallas_call(
        phase_kernel,
        grid=(4,),
        in_specs=[SMEM, pl.BlockSpec((CHANS, 128), lambda i: (0, i)), pl.BlockSpec((8, 128), lambda i: (0, 0))],
        out_specs=pl.BlockSpec((2, CHANS, 256), lambda i: (0, 0, i)),
        out_shape=pltpu.HBM((2, CHANS, 1024), BF16),
        compiler_params=LEAN,
        name="phases",
    )(numbers, delays, lut)


def search_kernel(f_ref, t_ref, o_ref):
    freq = f_ref[...].astype(F32).T.astype(BF16)
    sums = [jnp.dot(freq[pair * 64 : (pair + 1) * 64], t_ref[pair], preferred_element_type=F32) for pair in range(2)]
    for j in range(4):
        moved = []
        for pair in range(2):
            cos = sums[pair][:, j * 256 : j * 256 + 128]
            sin = sums[pair][:, j * 256 + 128 : j * 256 + 256]
            moved.append(cos[:32] - sin[32:])
            moved.append(sin[:32] + cos[32:])
        moved = jnp.concatenate(moved, axis=0) * (1.0 / math.sqrt(CHANS))
        o_ref[j * 128 : (j + 1) * 128, :] = moved.T.astype(BF16)


def search(freq, tables):
    return pl.pallas_call(
        search_kernel,
        in_specs=[VMEM, VMEM],
        out_specs=VMEM,
        out_shape=jax.ShapeDtypeStruct((512, 128), BF16),
        compiler_params=LEAN,
        name="search",
    )(freq, tables)


def local(voltages, feed_at_grid_slot, ew_grid, ns_grid, delays):
    tm = lax.axis_index(TIME)
    everyone = ("core", "z_hi", "z_lo", "y", "x")
    me = lax.axis_index(everyone)
    block = lax.axis_index(("z_lo", "y"))
    back, ahead = edges(in_hbm(voltages))
    back = lax.ppermute(back, TIME, [(i, i + 1) for i in range(15)])
    ahead = lax.ppermute(ahead, TIME, [((i + 1) % 16, i) for i in range(16)])
    window = pfb_window() * (1.0 / 64.0)
    keep = jnp.where(tm == 15, 0, 1).astype(jnp.int32).reshape(1)
    spectra = channelize(prefilter(keep, voltages, window), back, ahead, window, twiddle_tables())
    chan_ids = (me % 256) * 4 + me // 256 + 2 * jnp.arange(2, dtype=jnp.int32) + CHANS
    ew = steer_seed(jnp.arange(4, dtype=jnp.int32), ew_grid, chan_ids, 0.5)
    ew = jnp.stack([x.astype(BF16).astype(F32).transpose(0, 2, 1).reshape(32) for x in ew])
    forward, backward = time_rows()
    backward = backward.reshape(4, 2, 8, SPECTRA).transpose(0, 2, 1, 3).reshape(4, 16, SPECTRA)
    angles = jnp.arange(128, dtype=jnp.int32) % SPECTRA
    angles = angles.astype(F32) * (TWO_PI / SPECTRA)
    lut = jnp.stack([jnp.cos(angles), jnp.sin(angles)] + [jnp.zeros_like(angles)] * 6)
    numbers = jnp.stack([block + 1, jnp.where(block == 15, 1, 0)]).astype(jnp.int32)
    ns = north_tables(ns_grid, chan_ids)
    select = selection(feed_at_grid_slot.reshape(ROWS, 8).T)
    spectra, select, ns, ew, forward, backward, lut, numbers = lax.optimization_barrier(
        (spectra, select, ns, ew, forward, backward, lut, numbers)
    )
    received = lax.all_to_all(spectra, everyone, split_axis=0, concat_axis=0, tiled=True)
    freq = form_beams(received.reshape(2, 4, 16, 4, 8, 128), in_hbm(select), ns, ew, forward)
    freq, delays = lax.optimization_barrier((freq, delays))
    tables = phase_tables(numbers, delays, lut)
    by_freq = lax.all_to_all(freq.reshape(512, 2, 128), everyone, split_axis=0, concat_axis=0, tiled=True)
    moved = search(by_freq.reshape(CHANS, 128), tables)
    combined = lax.all_to_all(moved.reshape(16, 32, 128), TIME, split_axis=0, concat_axis=0, tiled=True)
    combined = combined.reshape(16, 32, 4, 32)
    return jnp.einsum("gdqb,qgt->dbt", combined, backward, preferred_element_type=F32)


def solution(mesh):
    split = Mesh(mesh.devices.reshape(8, 2, 4, 4, 2), ("y", "z_lo", "z_hi", "x", "core"))
    in_specs = (P(FEED, TIME), P(), P(), P(), P())
    return jax.shard_map(local, mesh=split, in_specs=in_specs, out_specs=P(TIME, FEED, None), check_vma=False)
```

```python
import math
from functools import partial

import jax
import jax.numpy as jnp
from jax import lax
from jax.experimental import pallas as pl
from jax.experimental.pallas import tpu as pltpu
from jax.sharding import Mesh, PartitionSpec as P

NFFT = 2048
CHANS = 1024
TAPS = 4
ROWS = 256
SPECTRA = 64
HALF = NFFT // 2
TWO_PI = 2.0 * math.pi
PHASE_MODULUS = 1048576
F32 = jnp.float32
TIME = ("y", "z_lo")
FEED = ("z_hi", "x", "core")
BF16 = jnp.bfloat16
NT = (((1,), (1,)), ((), ()))


VMEM = pl.BlockSpec(memory_space=pltpu.VMEM)
SMEM = pl.BlockSpec(memory_space=pltpu.SMEM)
LEAN = pltpu.CompilerParams(vmem_limit_bytes=24 << 20)


def iota(shape, axis):
    return lax.broadcasted_iota(jnp.int32, shape, axis)


def pfb_window():
    points = jnp.arange(TAPS * NFFT, dtype=F32) + 0.5
    start_offset = points / NFFT - TAPS / 2.0
    taper = 0.5 - 0.5 * jnp.cos(TWO_PI * points / (TAPS * NFFT))
    values = (jnp.sinc(start_offset) * taper).reshape(TAPS, NFFT)
    return values / jnp.sqrt(jnp.sum(values * values, axis=0, keepdims=True))


def twiddle_tables():
    coarse = iota((32, HALF), 0) * iota((32, HALF), 1) % 64
    coarse = coarse.astype(F32) * (TWO_PI / 64)
    shape = (2, 32, HALF)
    row = iota(shape, 1)
    chan = (row // 2) * 2 + iota(shape, 0)
    fine = (chan * iota(shape, 2) + (row % 2) * 512) % NFFT
    fine = fine.astype(F32) * (TWO_PI / NFFT)
    factor = 1.0 / math.sqrt(NFFT)
    seeds = (jnp.cos(coarse), jnp.sin(coarse), jnp.cos(fine) * factor, jnp.sin(fine) * factor)
    cos_a, sin_a, cos_b, sin_b = lax.optimization_barrier(seeds)
    table = cos_a[None, :, None, :] * cos_b[:, None] - sin_a[None, :, None, :] * sin_b[:, None]
    return table.astype(BF16).reshape(2, 1024, HALF)


def steer_seed(steps, grid_ids, chan_ids, factor):
    phases = steps[None, :, None] * grid_ids[None, None, :] * chan_ids[:, None, None] % PHASE_MODULUS
    angles = phases.astype(F32) * (TWO_PI / PHASE_MODULUS)
    return jnp.cos(angles) * factor, jnp.sin(angles) * factor


def north_tables(ns_grid, chan_ids):
    steps = jnp.arange(16, dtype=jnp.int32)
    seeds = steer_seed(steps * 16, ns_grid, chan_ids, 1.0) + steer_seed(steps, ns_grid, chan_ids, 1.0 / math.sqrt(ROWS))
    cos_a, sin_a, cos_b, sin_b = lax.optimization_barrier(seeds)
    cos_a, sin_a = cos_a[:, :, None, :], sin_a[:, :, None, :]
    cos_b, sin_b = cos_b[:, None], sin_b[:, None]
    real = (cos_a * cos_b - sin_a * sin_b).astype(BF16).reshape(2, ROWS, 256)
    imag = (sin_a * cos_b + cos_a * sin_b).astype(BF16).reshape(2, ROWS, 256)
    return jnp.concatenate([real, imag], axis=2)


def time_rows():
    block = jnp.arange(16, dtype=jnp.int32)
    ks = jnp.stack([block + 1, jnp.where(block == 15, 32, 31 - block)])
    product = ks[:, :, None] * jnp.arange(SPECTRA, dtype=jnp.int32) % SPECTRA
    angles = product.astype(F32) * (TWO_PI / SPECTRA)
    factor = 1.0 / math.sqrt(SPECTRA)
    table = jnp.stack([jnp.cos(angles) * factor, -jnp.sin(angles) * factor], axis=1)
    weight = jnp.where(ks == 32, 1.0, 2.0)[:, None, :, None]
    table = table.astype(BF16)
    return table.reshape(64, SPECTRA), (table * weight.astype(BF16)).reshape(4, 16, SPECTRA)


def in_hbm(x):
    return pltpu.with_memory_space_constraint(x, pltpu.HBM)


def prefilter_kernel(v_ref, w_ref, o_ref):
    for s in range(4):
        total = None
        for at in range(s + 1):
            frame = v_ref[:, at * NFFT : (at + 1) * NFFT].astype(F32)
            tap = at - s + 3
            term = w_ref[tap : tap + 1, :] * frame
            total = term if total is None else total + term
        o_ref[s] = total


def prefilter(voltages, window):
    return pl.pallas_call(
        prefilter_kernel,
        in_specs=[VMEM, VMEM],
        out_specs=VMEM,
        out_shape=jax.ShapeDtypeStruct((4, 64, NFFT), F32),
        compiler_params=LEAN,
        name="prefilter",
    )(voltages, window)


def channelize_kernel(p_ref, h_ref, w_ref, t_ref, o_ref, x_ref):
    def filter_rows(i, _):
        at = pl.ds(pl.multiple_of(i * 16, 16), 16)
        for s in range(4):
            for half in range(2):
                parts = []
                for sign in range(2):
                    first = sign * HALF + half * 512
                    total = p_ref[s, at, first : first + 512]
                    for frame in range(s, 3):
                        tap = frame - s
                        lanes = frame * NFFT + first
                        total = total + w_ref[tap : tap + 1, first : first + 512] * h_ref[
                            at, lanes : lanes + 512
                        ].astype(F32)
                    parts.append(total)
                to = pl.ds(pl.multiple_of(s * 64 + i * 16, 16), 16)
                x_ref[0, to, half * 512 : half * 512 + 512] = (parts[0] + parts[1]).astype(BF16)
                x_ref[1, to, half * 512 : half * 512 + 512] = (parts[0] - parts[1]).astype(BF16)
        return 0

    lax.fori_loop(0, 4, filter_rows, 0)
    upper = iota((64, 8, 128), 1) < 4

    def transform(i, _):
        acc = lax.dot_general(t_ref[i], x_ref[i // 2], NT, preferred_element_type=F32)
        first = acc[:, :128].reshape(64, 8, 128)
        second = acc[:, 128:].reshape(64, 8, 128)
        at = pl.ds(pl.multiple_of(i * 64, 64), 64)
        o_ref[at, 0] = jnp.where(upper, first, pltpu.roll(second, 4, 1)).astype(BF16)
        o_ref[at, 1] = jnp.where(upper, pltpu.roll(first, 4, 1), second).astype(BF16)
        return 0

    lax.fori_loop(0, 4, transform, 0)


def channelize(partial_sums, halo, window, table):
    out = pl.pallas_call(
        channelize_kernel,
        in_specs=[VMEM] * 4,
        out_specs=VMEM,
        out_shape=jax.ShapeDtypeStruct((256, 2, 8, 128), BF16),
        scratch_shapes=[pltpu.VMEM((2, 256, HALF), BF16)],
        compiler_params=LEAN,
        name="channelize",
    )(partial_sums, halo, window, table.reshape(4, 512, HALF))
    return out.reshape(512, 8, 128)


def select_kernel(slot_ref, o_ref):
    slots = slot_ref[pl.ds(pl.program_id(0), 1), :]

    def rows(j, _):
        at = pl.ds(pl.multiple_of(j * 256, 256), 256)
        feed = iota((256, 256), 0) + j * 256
        o_ref[0, at, :] = jnp.where(feed == slots, 1.0, 0.0).astype(BF16)
        return 0

    lax.fori_loop(0, 8, rows, 0)


def selection(slots):
    return pl.pallas_call(
        select_kernel,
        grid=(8,),
        in_specs=[VMEM],
        out_specs=pl.BlockSpec((1, 2048, 256), lambda i: (i, 0, 0)),
        out_shape=pltpu.HBM((8, 2048, 256), BF16),
        compiler_params=LEAN,
        name="selection",
    )(slots)


def beam_kernel(r_ref, select_ref, ns_ref, ew_ref, time_ref, o_ref, x_ref, y_ref, z_ref, s_ref):
    @pl.when(pl.program_id(0) == 0)
    def _():
        left = iota((128, 128), 1) < 64

        def assemble(g, _):
            first = r_ref[0, g // 4, :, g % 4].astype(F32).reshape(128, 128)
            second = r_ref[1, g // 4, :, g % 4].astype(F32).reshape(128, 128)
            lanes = pl.ds(pl.multiple_of(g * 128, 128), 128)
            z_ref[0:128, lanes] = jnp.where(left, first, pltpu.roll(second, 64, 1)).astype(BF16)
            z_ref[128:256, lanes] = jnp.where(left, pltpu.roll(first, 64, 1), second).astype(BF16)
            return 0

        lax.fori_loop(0, 16, assemble, 0)
        row = iota((256, 256), 0)
        time = row % 64
        source = (time % 2) * 128 + ((time // 4) % 2) * 64 + (time // 8) * 8 + ((time // 2) % 2) * 4 + row // 64
        order = jnp.where(source == iota((256, 256), 1), 1.0, 0.0).astype(BF16)
        x_ref[...] = jnp.dot(order, z_ref[...], preferred_element_type=F32).astype(BF16)

    grids = [jnp.dot(x_ref[...], select_ref[pol], preferred_element_type=F32).astype(BF16) for pol in range(2)]
    cyl = pl.program_id(0)
    for c in range(2):
        rows = jnp.concatenate([grid[c * 128 : (c + 1) * 128] for grid in grids], axis=0)
        both = jnp.dot(rows, ns_ref[c], preferred_element_type=F32)
        for pol in range(2):
            y_ref[c, cyl, pol, 0] = both[pol * 128 : pol * 128 + 64, :256] - both[pol * 128 + 64 : pol * 128 + 128, 256:]
            y_ref[c, cyl, pol, 1] = both[pol * 128 + 64 : pol * 128 + 128, :256] + both[pol * 128 : pol * 128 + 64, 256:]

    @pl.when(pl.program_id(0) == 3)
    def _():
        quarter = iota((16, 128), 1) // 32
        for c in range(2):

            def east_beam(e):
                power = None
                for pol in range(2):
                    real = 0.5 * y_ref[c, 0, pol, 0]
                    imag = 0.5 * y_ref[c, 0, pol, 1]
                    for cyl in range(1, 4):
                        w_re = ew_ref[0, c * 16 + e * 4 + cyl]
                        w_im = ew_ref[1, c * 16 + e * 4 + cyl]
                        y_re = y_ref[c, cyl, pol, 0]
                        y_im = y_ref[c, cyl, pol, 1]
                        real = real + (w_re * y_re - w_im * y_im)
                        imag = imag + (w_re * y_im + w_im * y_re)
                    part = real * real + imag * imag
                    power = part if power is None else power + part
                freq = jnp.dot(time_ref[...], power.astype(BF16), preferred_element_type=F32)
                freq = freq.reshape(4, 16, 256)
                for half in range(2):
                    part = freq[:, :, half * 128 : (half + 1) * 128]
                    turned = [part] + [pltpu.roll(part, 32 * n, 2) for n in range(1, 4)]
                    for low in range(4):
                        rows = turned[-low % 4][0]
                        for q in range(1, 4):
                            rows = jnp.where(quarter == q, turned[(q - low) % 4][q], rows)
                        bh = half * 4 + low
                        start = ((bh % 2) * 256 + e * 64 + bh // 2) * 2 + c
                        s_ref[pl.ds(start, 16, stride=8), :] = rows

            def east(i, _):
                east_beam(2 * i)
                east_beam(2 * i + 1)
                return 0

            lax.fori_loop(0, 2, east, 0)
        o_ref[...] = s_ref[...].astype(BF16)


def form_beams(received, select, ns_table, ew_table, time_table):
    return pl.pallas_call(
        beam_kernel,
        grid=(4,),
        in_specs=[VMEM, pl.BlockSpec((2, 2048, 256), lambda i: (i, 0, 0)), VMEM, SMEM, VMEM],
        out_specs=VMEM,
        out_shape=jax.ShapeDtypeStruct((1024, 128), BF16),
        scratch_shapes=[
            pltpu.VMEM((256, 2048), BF16),
            pltpu.VMEM((2, 4, 2, 2, 64, 256), F32),
            pltpu.VMEM((256, 2048), BF16),
            pltpu.VMEM((1024, 128), F32),
        ],
        compiler_params=LEAN,
        name="beams",
    )(received, select, ns_table, ew_table, time_table)


def phase_kernel(num_ref, d_ref, lut_ref, o_ref):
    first_k = num_ref[0]
    plain = num_ref[1].astype(F32)
    scale = 1.0 - plain
    cos_lut = jnp.broadcast_to(lut_ref[0:1, :], (256, 128))
    sin_lut = jnp.broadcast_to(lut_ref[1:2, :], (256, 128))
    for parity in range(2):

        def fill(i, _):
            at = pl.ds(pl.multiple_of(parity * 512 + i * 256, 256), 256)
            delays = d_ref[pl.ds(i * 512 + parity, 256, stride=2), :]
            turn = (first_k * delays) & (SPECTRA - 1)
            cos = jnp.take_along_axis(cos_lut, turn, axis=1)
            sin = jnp.take_along_axis(sin_lut, turn, axis=1)
            sign = (1 - 2 * (delays & 1)).astype(F32)
            o_ref[0, at, :128] = cos.astype(BF16)
            o_ref[0, at, 128:] = sin.astype(BF16)
            o_ref[1, at, :128] = (sign * (plain + scale * cos)).astype(BF16)
            o_ref[1, at, 128:] = (-scale * sign * sin).astype(BF16)
            return 0

        lax.fori_loop(0, 2, fill, 0)


def phase_tables(numbers, delays, lut):
    return pl.pallas_call(
        phase_kernel,
        grid=(4,),
        in_specs=[SMEM, pl.BlockSpec((CHANS, 128), lambda i: (0, i)), pl.BlockSpec((8, 128), lambda i: (0, 0))],
        out_specs=pl.BlockSpec((2, CHANS, 256), lambda i: (0, 0, i)),
        out_shape=pltpu.HBM((2, CHANS, 1024), BF16),
        compiler_params=LEAN,
        name="phases",
    )(numbers, delays, lut)


def search_kernel(f_ref, t_ref, o_ref):
    freq = f_ref[...].astype(F32).T.astype(BF16)
    sums = [jnp.dot(freq[pair * 64 : (pair + 1) * 64], t_ref[pair], preferred_element_type=F32) for pair in range(2)]
    for j in range(4):
        moved = []
        for pair in range(2):
            cos = sums[pair][:, j * 256 : j * 256 + 128]
            sin = sums[pair][:, j * 256 + 128 : j * 256 + 256]
            moved.append(cos[:32] - sin[32:])
            moved.append(sin[:32] + cos[32:])
        moved = jnp.concatenate(moved, axis=0) * (1.0 / math.sqrt(CHANS))
        o_ref[j * 128 : (j + 1) * 128, :] = moved.T.astype(BF16)


def search(freq, tables):
    return pl.pallas_call(
        search_kernel,
        in_specs=[VMEM, VMEM],
        out_specs=VMEM,
        out_shape=jax.ShapeDtypeStruct((512, 128), BF16),
        compiler_params=LEAN,
        name="search",
    )(freq, tables)


def local(voltages, feed_at_grid_slot, ew_grid, ns_grid, delays):
    everyone = ("core", "z_hi", "z_lo", "y", "x")
    me = lax.axis_index(everyone)
    block = lax.axis_index(("z_lo", "y"))
    tail = voltages[:, NFFT:].astype(BF16)
    halo = lax.ppermute(tail, TIME, [(i, i + 1) for i in range(15)])
    window = pfb_window() * (1.0 / 64.0)
    spectra = channelize(prefilter(voltages, window), halo, window, twiddle_tables())
    received = lax.all_to_all(spectra, everyone, split_axis=0, concat_axis=0, tiled=True)

    chan_ids = (me % 256) * 4 + me // 256 + 2 * jnp.arange(2, dtype=jnp.int32) + CHANS
    ew = steer_seed(jnp.arange(4, dtype=jnp.int32), ew_grid, chan_ids, 0.5)
    ew = jnp.stack([x.astype(BF16).astype(F32).transpose(0, 2, 1).reshape(32) for x in ew])
    slots = feed_at_grid_slot.reshape(ROWS, 8).T
    forward, backward = time_rows()
    angles = jnp.arange(128, dtype=jnp.int32) % SPECTRA
    angles = angles.astype(F32) * (TWO_PI / SPECTRA)
    lut = jnp.stack([jnp.cos(angles), jnp.sin(angles)] + [jnp.zeros_like(angles)] * 6)
    numbers = jnp.stack([block + 1, jnp.where(block == 15, 1, 0)]).astype(jnp.int32)
    tables = phase_tables(numbers, delays, lut)
    received, tables = lax.optimization_barrier((received, tables))
    select = pltpu.with_memory_space_constraint(selection(slots), pltpu.HBM)
    freq = form_beams(
        received.reshape(2, 4, 16, 4, 8, 128), select, north_tables(ns_grid, chan_ids), ew, forward
    )
    by_freq = lax.all_to_all(freq.reshape(512, 2, 128), everyone, split_axis=0, concat_axis=0, tiled=True)
    moved = search(by_freq.reshape(CHANS, 128), tables)
    combined = lax.all_to_all(moved.reshape(16, 32, 128), TIME, split_axis=0, concat_axis=0, tiled=True)
    combined = combined.reshape(16, 32, 4, 32)
    backward = backward.reshape(4, 2, 8, SPECTRA).transpose(0, 2, 1, 3).reshape(4, 16, SPECTRA)
    return jnp.einsum("gdqb,qgt->dbt", combined, backward, preferred_element_type=F32)


def solution(mesh):
    split = Mesh(mesh.devices.reshape(8, 2, 4, 4, 2), ("y", "z_lo", "z_hi", "x", "core"))
    in_specs = (P(FEED, TIME), P(), P(), P(), P())
    return jax.shard_map(local, mesh=split, in_specs=in_specs, out_specs=P(TIME, FEED, None), check_vma=False)
```

```python
import math
from functools import partial

import jax
import jax.numpy as jnp
from jax import lax
from jax.experimental import pallas as pl
from jax.experimental.pallas import tpu as pltpu
from jax.sharding import Mesh, PartitionSpec as P

NFFT = 2048
CHANS = 1024
TAPS = 4
ROWS = 256
SPECTRA = 64
HALF = NFFT // 2
TWO_PI = 2.0 * math.pi
PHASE_MODULUS = 1048576
F32 = jnp.float32
TIME = ("y", "z_lo")
FEED = ("z_hi", "x", "core")
BF16 = jnp.bfloat16
NT = (((1,), (1,)), ((), ()))


VMEM = pl.BlockSpec(memory_space=pltpu.VMEM)
SMEM = pl.BlockSpec(memory_space=pltpu.SMEM)
LEAN = pltpu.CompilerParams(vmem_limit_bytes=24 << 20)


def iota(shape, axis):
    return lax.broadcasted_iota(jnp.int32, shape, axis)


def pfb_window():
    points = jnp.arange(TAPS * NFFT, dtype=F32) + 0.5
    start_offset = points / NFFT - TAPS / 2.0
    taper = 0.5 - 0.5 * jnp.cos(TWO_PI * points / (TAPS * NFFT))
    values = (jnp.sinc(start_offset) * taper).reshape(TAPS, NFFT)
    return values / jnp.sqrt(jnp.sum(values * values, axis=0, keepdims=True))


def twiddle_tables():
    coarse = iota((32, HALF), 0) * iota((32, HALF), 1) % 64
    coarse = coarse.astype(F32) * (TWO_PI / 64)
    shape = (2, 32, HALF)
    row = iota(shape, 1)
    chan = (row // 2) * 2 + iota(shape, 0)
    fine = (chan * iota(shape, 2) + (row % 2) * 512) % NFFT
    fine = fine.astype(F32) * (TWO_PI / NFFT)
    factor = 1.0 / math.sqrt(NFFT)
    seeds = (jnp.cos(coarse), jnp.sin(coarse), jnp.cos(fine) * factor, jnp.sin(fine) * factor)
    cos_a, sin_a, cos_b, sin_b = lax.optimization_barrier(seeds)
    table = cos_a[None, :, None, :] * cos_b[:, None] - sin_a[None, :, None, :] * sin_b[:, None]
    return table.astype(BF16).reshape(2, 1024, HALF)


def steer_seed(steps, grid_ids, chan_ids, factor):
    phases = steps[None, :, None] * grid_ids[None, None, :] * chan_ids[:, None, None] % PHASE_MODULUS
    angles = phases.astype(F32) * (TWO_PI / PHASE_MODULUS)
    return jnp.cos(angles) * factor, jnp.sin(angles) * factor


def north_tables(ns_grid, chan_ids):
    steps = jnp.arange(16, dtype=jnp.int32)
    seeds = steer_seed(steps * 16, ns_grid, chan_ids, 1.0) + steer_seed(steps, ns_grid, chan_ids, 1.0 / math.sqrt(ROWS))
    cos_a, sin_a, cos_b, sin_b = lax.optimization_barrier(seeds)
    cos_a, sin_a = cos_a[:, :, None, :], sin_a[:, :, None, :]
    cos_b, sin_b = cos_b[:, None], sin_b[:, None]
    real = (cos_a * cos_b - sin_a * sin_b).astype(BF16).reshape(2, ROWS, 256)
    imag = (sin_a * cos_b + cos_a * sin_b).astype(BF16).reshape(2, ROWS, 256)
    return jnp.concatenate([real, imag], axis=2)


def time_rows():
    block = jnp.arange(16, dtype=jnp.int32)
    ks = jnp.stack([block + 1, jnp.where(block == 15, 32, 31 - block)])
    product = ks[:, :, None] * jnp.arange(SPECTRA, dtype=jnp.int32) % SPECTRA
    angles = product.astype(F32) * (TWO_PI / SPECTRA)
    factor = 1.0 / math.sqrt(SPECTRA)
    table = jnp.stack([jnp.cos(angles) * factor, -jnp.sin(angles) * factor], axis=1)
    weight = jnp.where(ks == 32, 1.0, 2.0)[:, None, :, None]
    table = table.astype(BF16)
    return table.reshape(64, SPECTRA), (table * weight.astype(BF16)).reshape(4, 16, SPECTRA)


def in_hbm(x):
    return pltpu.with_memory_space_constraint(x, pltpu.HBM)


def prefilter_kernel(v_ref, w_ref, o_ref):
    for s in range(4):
        total = None
        for at in range(s + 1):
            frame = v_ref[:, at * NFFT : (at + 1) * NFFT].astype(F32)
            tap = at - s + 3
            term = w_ref[tap : tap + 1, :] * frame
            total = term if total is None else total + term
        o_ref[s] = total


def prefilter(voltages, window):
    return pl.pallas_call(
        prefilter_kernel,
        in_specs=[VMEM, VMEM],
        out_specs=VMEM,
        out_shape=jax.ShapeDtypeStruct((4, 64, NFFT), F32),
        compiler_params=LEAN,
        name="prefilter",
    )(voltages, window)


def channelize_kernel(p_ref, h_ref, w_ref, t_ref, o_ref, x_ref):
    def filter_rows(i, _):
        at = pl.ds(pl.multiple_of(i * 16, 16), 16)
        for s in range(4):
            for half in range(2):
                parts = []
                for sign in range(2):
                    first = sign * HALF + half * 512
                    total = p_ref[s, at, first : first + 512]
                    for frame in range(s, 3):
                        tap = frame - s
                        lanes = frame * NFFT + first
                        total = total + w_ref[tap : tap + 1, first : first + 512] * h_ref[
                            at, lanes : lanes + 512
                        ].astype(F32)
                    parts.append(total)
                to = pl.ds(pl.multiple_of(s * 64 + i * 16, 16), 16)
                x_ref[0, to, half * 512 : half * 512 + 512] = (parts[0] + parts[1]).astype(BF16)
                x_ref[1, to, half * 512 : half * 512 + 512] = (parts[0] - parts[1]).astype(BF16)
        return 0

    lax.fori_loop(0, 4, filter_rows, 0)
    upper = iota((64, 8, 128), 1) < 4

    def transform(i, _):
        acc = lax.dot_general(t_ref[i], x_ref[i // 2], NT, preferred_element_type=F32)
        first = acc[:, :128].reshape(64, 8, 128)
        second = acc[:, 128:].reshape(64, 8, 128)
        at = pl.ds(pl.multiple_of(i * 64, 64), 64)
        o_ref[at, 0] = jnp.where(upper, first, pltpu.roll(second, 4, 1)).astype(BF16)
        o_ref[at, 1] = jnp.where(upper, pltpu.roll(first, 4, 1), second).astype(BF16)
        return 0

    lax.fori_loop(0, 4, transform, 0)


def channelize(partial_sums, halo, window, table):
    out = pl.pallas_call(
        channelize_kernel,
        in_specs=[VMEM] * 4,
        out_specs=VMEM,
        out_shape=jax.ShapeDtypeStruct((256, 2, 8, 128), BF16),
        scratch_shapes=[pltpu.VMEM((2, 256, HALF), BF16)],
        compiler_params=LEAN,
        name="channelize",
    )(partial_sums, halo, window, table.reshape(4, 512, HALF))
    return out.reshape(512, 8, 128)


def select_kernel(slot_ref, o_ref):
    slots = jnp.concatenate([slot_ref[pl.ds(2 * pl.program_id(0) + pol, 1), :] for pol in range(2)], axis=1)

    def rows(j, _):
        at = pl.ds(pl.multiple_of(j * 256, 256), 256)
        feed = iota((256, 512), 0) + j * 256
        o_ref[0, at, :] = jnp.where(feed == slots, 1.0, 0.0).astype(BF16)
        return 0

    lax.fori_loop(0, 8, rows, 0)


def selection(slots):
    return pl.pallas_call(
        select_kernel,
        grid=(4,),
        in_specs=[VMEM],
        out_specs=pl.BlockSpec((1, 2048, 512), lambda i: (i, 0, 0)),
        out_shape=pltpu.HBM((4, 2048, 512), BF16),
        compiler_params=LEAN,
        name="selection",
    )(slots)


def beam_kernel(r_ref, select_ref, ns_ref, ew_ref, time_ref, o_ref, x_ref, y_ref, z_ref, s_ref):
    @pl.when(pl.program_id(0) == 0)
    def _():
        left = iota((128, 128), 1) < 64

        def assemble(g, _):
            first = r_ref[0, g // 4, :, g % 4].astype(F32).reshape(128, 128)
            second = r_ref[1, g // 4, :, g % 4].astype(F32).reshape(128, 128)
            lanes = pl.ds(pl.multiple_of(g * 128, 128), 128)
            z_ref[0:128, lanes] = jnp.where(left, first, pltpu.roll(second, 64, 1)).astype(BF16)
            z_ref[128:256, lanes] = jnp.where(left, pltpu.roll(first, 64, 1), second).astype(BF16)
            return 0

        lax.fori_loop(0, 16, assemble, 0)
        row = iota((256, 256), 0)
        time = row % 64
        source = (time % 2) * 128 + ((time // 4) % 2) * 64 + (time // 8) * 8 + ((time // 2) % 2) * 4 + row // 64
        order = jnp.where(source == iota((256, 256), 1), 1.0, 0.0).astype(BF16)
        x_ref[...] = jnp.dot(order, z_ref[...], preferred_element_type=F32).astype(BF16)

    both_pol = jnp.dot(x_ref[...], select_ref[0], preferred_element_type=F32).astype(BF16)
    grids = [both_pol[:, :256], both_pol[:, 256:]]
    cyl = pl.program_id(0)
    for c in range(2):
        rows = jnp.concatenate([grid[c * 128 : (c + 1) * 128] for grid in grids], axis=0)
        both = jnp.dot(rows, ns_ref[c], preferred_element_type=F32)
        for pol in range(2):
            y_ref[c, cyl, pol, 0] = both[pol * 128 : pol * 128 + 64, :256] - both[pol * 128 + 64 : pol * 128 + 128, 256:]
            y_ref[c, cyl, pol, 1] = both[pol * 128 + 64 : pol * 128 + 128, :256] + both[pol * 128 : pol * 128 + 64, 256:]

    @pl.when(pl.program_id(0) == 3)
    def _():
        quarter = iota((16, 128), 1) // 32
        for c in range(2):

            def east_beam(e):
                power = None
                for pol in range(2):
                    real = 0.5 * y_ref[c, 0, pol, 0]
                    imag = 0.5 * y_ref[c, 0, pol, 1]
                    for cyl in range(1, 4):
                        w_re = ew_ref[0, c * 16 + e * 4 + cyl]
                        w_im = ew_ref[1, c * 16 + e * 4 + cyl]
                        y_re = y_ref[c, cyl, pol, 0]
                        y_im = y_ref[c, cyl, pol, 1]
                        real = real + (w_re * y_re - w_im * y_im)
                        imag = imag + (w_re * y_im + w_im * y_re)
                    part = real * real + imag * imag
                    power = part if power is None else power + part
                freq = jnp.dot(time_ref[...], power.astype(BF16), preferred_element_type=F32)
                freq = freq.reshape(4, 16, 256)
                for half in range(2):
                    part = freq[:, :, half * 128 : (half + 1) * 128]
                    turned = [part] + [pltpu.roll(part, 32 * n, 2) for n in range(1, 4)]
                    for low in range(4):
                        rows = turned[-low % 4][0]
                        for q in range(1, 4):
                            rows = jnp.where(quarter == q, turned[(q - low) % 4][q], rows)
                        bh = half * 4 + low
                        start = ((bh % 2) * 256 + e * 64 + bh // 2) * 2 + c
                        s_ref[pl.ds(start, 16, stride=8), :] = rows

            def east(i, _):
                east_beam(2 * i)
                east_beam(2 * i + 1)
                return 0

            lax.fori_loop(0, 2, east, 0)
        o_ref[...] = s_ref[...].astype(BF16)


def form_beams(received, select, ns_table, ew_table, time_table):
    return pl.pallas_call(
        beam_kernel,
        grid=(4,),
        in_specs=[VMEM, pl.BlockSpec((1, 2048, 512), lambda i: (i, 0, 0)), VMEM, SMEM, VMEM],
        out_specs=VMEM,
        out_shape=jax.ShapeDtypeStruct((1024, 128), BF16),
        scratch_shapes=[
            pltpu.VMEM((256, 2048), BF16),
            pltpu.VMEM((2, 4, 2, 2, 64, 256), F32),
            pltpu.VMEM((256, 2048), BF16),
            pltpu.VMEM((1024, 128), F32),
        ],
        compiler_params=LEAN,
        name="beams",
    )(received, select, ns_table, ew_table, time_table)


def phase_kernel(num_ref, d_ref, lut_ref, o_ref):
    first_k = num_ref[0]
    plain = num_ref[1].astype(F32)
    scale = 1.0 - plain
    cos_lut = jnp.broadcast_to(lut_ref[0:1, :], (256, 128))
    sin_lut = jnp.broadcast_to(lut_ref[1:2, :], (256, 128))
    for parity in range(2):

        def fill(i, _):
            at = pl.ds(pl.multiple_of(parity * 512 + i * 256, 256), 256)
            delays = d_ref[pl.ds(i * 512 + parity, 256, stride=2), :]
            turn = (first_k * delays) & (SPECTRA - 1)
            cos = jnp.take_along_axis(cos_lut, turn, axis=1)
            sin = jnp.take_along_axis(sin_lut, turn, axis=1)
            sign = (1 - 2 * (delays & 1)).astype(F32)
            o_ref[0, at, :128] = cos.astype(BF16)
            o_ref[0, at, 128:] = sin.astype(BF16)
            o_ref[1, at, :128] = (sign * (plain + scale * cos)).astype(BF16)
            o_ref[1, at, 128:] = (-scale * sign * sin).astype(BF16)
            return 0

        lax.fori_loop(0, 2, fill, 0)


def phase_tables(numbers, delays, lut):
    return pl.pallas_call(
        phase_kernel,
        grid=(4,),
        in_specs=[SMEM, pl.BlockSpec((CHANS, 128), lambda i: (0, i)), pl.BlockSpec((8, 128), lambda i: (0, 0))],
        out_specs=pl.BlockSpec((2, CHANS, 256), lambda i: (0, 0, i)),
        out_shape=pltpu.HBM((2, CHANS, 1024), BF16),
        compiler_params=LEAN,
        name="phases",
    )(numbers, delays, lut)


def search_kernel(f_ref, t_ref, o_ref):
    freq = f_ref[...].astype(F32).T.astype(BF16)
    sums = [jnp.dot(freq[pair * 64 : (pair + 1) * 64], t_ref[pair], preferred_element_type=F32) for pair in range(2)]
    for j in range(4):
        moved = []
        for pair in range(2):
            cos = sums[pair][:, j * 256 : j * 256 + 128]
            sin = sums[pair][:, j * 256 + 128 : j * 256 + 256]
            moved.append(cos[:32] - sin[32:])
            moved.append(sin[:32] + cos[32:])
        moved = jnp.concatenate(moved, axis=0) * (1.0 / math.sqrt(CHANS))
        o_ref[j * 128 : (j + 1) * 128, :] = moved.T.astype(BF16)


def search(freq, tables):
    return pl.pallas_call(
        search_kernel,
        in_specs=[VMEM, VMEM],
        out_specs=VMEM,
        out_shape=jax.ShapeDtypeStruct((512, 128), BF16),
        compiler_params=LEAN,
        name="search",
    )(freq, tables)


def local(voltages, feed_at_grid_slot, ew_grid, ns_grid, delays):
    everyone = ("core", "z_hi", "z_lo", "y", "x")
    me = lax.axis_index(everyone)
    block = lax.axis_index(("z_lo", "y"))
    tail = voltages[:, NFFT:].astype(BF16)
    halo = lax.ppermute(tail, TIME, [(i, i + 1) for i in range(15)])
    window = pfb_window() * (1.0 / 64.0)
    spectra = channelize(prefilter(voltages, window), halo, window, twiddle_tables())
    received = lax.all_to_all(spectra, everyone, split_axis=0, concat_axis=0, tiled=True)

    chan_ids = (me % 256) * 4 + me // 256 + 2 * jnp.arange(2, dtype=jnp.int32) + CHANS
    ew = steer_seed(jnp.arange(4, dtype=jnp.int32), ew_grid, chan_ids, 0.5)
    ew = jnp.stack([x.astype(BF16).astype(F32).transpose(0, 2, 1).reshape(32) for x in ew])
    slots = feed_at_grid_slot.reshape(ROWS, 8).T
    forward, backward = time_rows()
    angles = jnp.arange(128, dtype=jnp.int32) % SPECTRA
    angles = angles.astype(F32) * (TWO_PI / SPECTRA)
    lut = jnp.stack([jnp.cos(angles), jnp.sin(angles)] + [jnp.zeros_like(angles)] * 6)
    numbers = jnp.stack([block + 1, jnp.where(block == 15, 1, 0)]).astype(jnp.int32)
    tables = phase_tables(numbers, delays, lut)
    received, tables = lax.optimization_barrier((received, tables))
    select = pltpu.with_memory_space_constraint(selection(slots), pltpu.HBM)
    freq = form_beams(
        received.reshape(2, 4, 16, 4, 8, 128), select, north_tables(ns_grid, chan_ids), ew, forward
    )
    by_freq = lax.all_to_all(freq.reshape(512, 2, 128), everyone, split_axis=0, concat_axis=0, tiled=True)
    moved = search(by_freq.reshape(CHANS, 128), tables)
    combined = lax.all_to_all(moved.reshape(16, 32, 128), TIME, split_axis=0, concat_axis=0, tiled=True)
    combined = combined.reshape(16, 32, 4, 32)
    backward = backward.reshape(4, 2, 8, SPECTRA).transpose(0, 2, 1, 3).reshape(4, 16, SPECTRA)
    return jnp.einsum("gdqb,qgt->dbt", combined, backward, preferred_element_type=F32)


def solution(mesh):
    split = Mesh(mesh.devices.reshape(8, 2, 4, 4, 2), ("y", "z_lo", "z_hi", "x", "core"))
    in_specs = (P(FEED, TIME), P(), P(), P(), P())
    return jax.shard_map(local, mesh=split, in_specs=in_specs, out_specs=P(TIME, FEED, None), check_vma=False)
```
